32 devices in a mesh: member: 4 (over y, x), domain: 8 (over z, core).
Axes of the slice: x: 2, y: 2, z: 4, core: 2. Of those that a mesh axis runs over, the one named last changes fastest.
Arguments:
- ensemble: float32 [80, 4, 3, 16, 2048], P('member', None, None, None, 'domain'), may hold values from -9 to 9
- velocity: float32 [2, 3, 16, 2048], P(None, None, None, 'domain'), may hold values from -0.5 to 0.5
- diffusivity: float32 [4], replicated, may hold values from 0.05 to 0.2
- land_mask: int32 [16, 2048], P(None, 'domain'), may hold values from 0 to 1
- obs_index: int32 [4, 8, 4], replicated, may hold values from 0 to 255, as said below
- obs_owner: int32 [4], replicated, may hold values from 0 to 31, as said below
- obs_value: float32 [4, 8], replicated, may hold values from -4 to 4
- obs_error: float32 [4, 8], replicated, may hold values from 0.2 to 1
Outputs:
- analysis: float32 [80, 4, 3, 16, 2048], P(None, None, None, 'member', 'domain')
The draws below stay inside these ranges and needn't reach their ends.
Inputs may be any that keep to these rules, and one draw needn't show every extreme that they name: `obs_index`: each observed cell has land_mask 1. The first observation of batch 0 is field 0, level 0 at its block's first row and column; the last observation of batch 3 is field 3, level 2 at its block's last row and column. A device's number is its member index times the number of domain tiles plus its domain index. obs_owner[0] is the first device and obs_owner[3] the last.
All inputs are finite; a program needn't handle non-finite values.
Results may differ from the reference program's by a relative error of at most 0.0001.
Values sent between devices are 32-bit elements; how exact they have to be, the bound alone decides.
No kernel may reach another device: no remote copies, remote signals or barrier semaphores. Data moves between devices by JAX's collectives and lax.ppermute only.
A program may use at most 192 MiB of HBM per device.

```python
import math
import jax
import jax.numpy as jnp
from jax import lax

MEMBERS = 80
FIELDS = 4
LEVELS = 3
ROWS = 16
COLS_DEV = 256
BATCHES = 4
OBS_BATCH = 8
LOC_RADIUS = 64
ROWS_DEV = 4
COLS = 2048
N_DOMAIN = 8


def observation_tables(key):
    keys = jax.random.split(jax.random.fold_in(key, 101), 5)
    domain_total = COLS // COLS_DEV
    device_total = domain_total * (ROWS // ROWS_DEV)
    owner_dev = jax.random.randint(keys[0], (BATCHES,), 0, device_total, dtype=jnp.int32)
    owner_dev = owner_dev.at[0].set(0).at[BATCHES - 1].set(device_total - 1)
    local_row = jax.random.randint(keys[1], (BATCHES, OBS_BATCH), 0, ROWS_DEV, dtype=jnp.int32)
    local_row = local_row.at[0, 0].set(0).at[BATCHES - 1, OBS_BATCH - 1].set(ROWS_DEV - 1)
    local_col = jax.random.randint(keys[2], (BATCHES, OBS_BATCH), 0, COLS_DEV, dtype=jnp.int32)
    local_col = local_col.at[0, 0].set(0).at[BATCHES - 1, OBS_BATCH - 1].set(COLS_DEV - 1)
    field_num = jax.random.randint(keys[3], (BATCHES, OBS_BATCH), 0, FIELDS, dtype=jnp.int32)
    field_num = field_num.at[0, 0].set(0).at[BATCHES - 1, OBS_BATCH - 1].set(FIELDS - 1)
    level_num = jax.random.randint(keys[4], (BATCHES, OBS_BATCH), 0, LEVELS, dtype=jnp.int32)
    level_num = level_num.at[0, 0].set(0).at[BATCHES - 1, OBS_BATCH - 1].set(LEVELS - 1)
    table = jnp.stack([field_num, level_num, local_row, local_col], axis=-1).astype(jnp.int32)
    grid_row = (owner_dev // domain_total)[:, None] * ROWS_DEV + local_row
    grid_col = (owner_dev % domain_total)[:, None] * COLS_DEV + local_col
    return (owner_dev, table, grid_row, grid_col)


def draw_obs_owner(key, part):
    owner_dev, table, grid_row, grid_col = observation_tables(key)
    return owner_dev


def draw_obs_index(key, part):
    owner_dev, table, grid_row, grid_col = observation_tables(key)
    return table


def draw_land_mask(key, part):
    owner_dev, table, grid_row, grid_col = observation_tables(key)
    levels_drawn = jax.random.randint(jax.random.fold_in(key, 202), (ROWS, COLS), 0, 5, dtype=jnp.int32)
    ocean = (levels_drawn > 0).astype(jnp.int32)
    return ocean.at[grid_row.reshape(-1), grid_col.reshape(-1)].set(1)


def draw_ensemble(key, part):
    keys = jax.random.split(jax.random.fold_in(key, 303), 3)
    full_shape = (MEMBERS, FIELDS, LEVELS, ROWS, COLS)
    amplitude = jax.random.uniform(keys[2], (1, FIELDS, LEVELS, ROWS, COLS), jnp.float32, 0.5, 1.5)
    noise = jnp.clip(jax.random.normal(keys[0], full_shape, jnp.float32), -4.0, 4.0)
    common = jnp.clip(jax.random.normal(keys[1], (MEMBERS, FIELDS, 1, 1, 1), jnp.float32), -3.0, 3.0)
    return noise + common * amplitude


def shard_levels(own_key, dims, cuts, least, largest):
    level = 1.0
    for dim, shards_of in cuts:
        steps = jax.random.uniform(jax.random.fold_in(jax.random.fold_in(own_key, 6), dim), (shards_of,), jnp.float32, least / len(cuts), largest / len(cuts))
        level = level * jnp.repeat(jnp.exp(steps), dims[dim] // shards_of).reshape((-1,) + (1,) * (len(dims) - 1 - dim))
    return level


def centred(rng, dims, scale, most, kind=jnp.bfloat16):
    array = jax.random.normal(rng, dims, jnp.float32) * scale
    return jnp.minimum(jnp.maximum(array, -most), most).astype(kind)


def setup_inputs(seed: int = 0) -> dict:
    splits = jax.random.split(jax.random.key(seed), 9)
    ensemble = draw_ensemble(jax.random.fold_in(splits[8], 71), 0)
    velocity = jnp.clip(jax.random.uniform(splits[1], (2, LEVELS, ROWS, COLS), jnp.float32, -0.5, 0.5) * shard_levels(splits[1], (2, LEVELS, ROWS, COLS), ((3, 8),), -0.4, 0.0), -0.5, 0.5)
    diffusivity = jnp.clip(jnp.exp(jax.random.uniform(splits[2], (FIELDS,), jnp.float32, math.log(0.05), math.log(0.2))), 0.05, 0.2)
    land_mask = draw_land_mask(jax.random.fold_in(splits[8], 71), 0)
    obs_index = draw_obs_index(jax.random.fold_in(splits[8], 71), 0)
    obs_owner = draw_obs_owner(jax.random.fold_in(splits[8], 71), 0)
    obs_value = centred(splits[6], (BATCHES, OBS_BATCH), 1.0, 4.0, jnp.float32)
    obs_error = jnp.clip(jnp.exp(jax.random.uniform(splits[7], (BATCHES, OBS_BATCH), jnp.float32, math.log(0.2), math.log(1.0))), 0.2, 1.0)
    return dict(ensemble=ensemble, velocity=velocity, diffusivity=diffusivity, land_mask=land_mask, obs_index=obs_index, obs_owner=obs_owner, obs_value=obs_value, obs_error=obs_error)


def gaspari(distance, loc_radius):
    scaled = distance / loc_radius
    scaled_safe = jnp.maximum(scaled, 1.0)
    near_part = (((-0.25 * scaled + 0.5) * scaled + 0.625) * scaled - 5.0 / 3.0) * scaled * scaled + 1.0
    far_part = ((((scaled / 12.0 - 0.5) * scaled + 0.625) * scaled + 5.0 / 3.0) * scaled - 5.0) * scaled + 4.0 - 2.0 / (3.0 * scaled_safe)
    return jnp.where(scaled <= 1.0, near_part, jnp.where(scaled < 2.0, far_part, 0.0))

def separation(row_from, col_from, row_to, col_to, grid_width):
    col_gap = jnp.abs(col_from - col_to)
    col_gap = jnp.minimum(col_gap, grid_width - col_gap)
    row_gap = row_from - row_to
    return jnp.sqrt((col_gap * col_gap + row_gap * row_gap).astype(jnp.float32))

def advance(center, col_next, col_prev, row_next, row_prev, flow_u, flow_v, diffuse, wet_part):
    tendency = -flow_u * (col_next - col_prev) * 0.5 - flow_v * (row_next - row_prev) * 0.5 + diffuse * (col_next + col_prev + row_next + row_prev - 4.0 * center)
    return wet_part * (center + tendency)

def reference(ensemble, velocity, diffusivity, land_mask, obs_index, obs_owner, obs_value, obs_error):
    wet_all = land_mask.astype(jnp.float32)
    col_next = jnp.roll(ensemble, -1, axis=4)
    col_prev = jnp.roll(ensemble, 1, axis=4)
    zero_row = jnp.zeros_like(ensemble[:, :, :, :1, :])
    row_next = jnp.concatenate([ensemble[:, :, :, 1:, :], zero_row], axis=3)
    row_prev = jnp.concatenate([zero_row, ensemble[:, :, :, :-1, :]], axis=3)
    diffuse = diffusivity[None, :, None, None, None]
    current = advance(ensemble, col_next, col_prev, row_next, row_prev, velocity[0][None, None], velocity[1][None, None], diffuse, wet_all)
    levels_total = FIELDS * LEVELS
    flat_state = current.reshape(MEMBERS, -1)
    wet_cells = wet_all.reshape(-1)
    wet_flat = jnp.broadcast_to(wet_all[None], (levels_total, ROWS, COLS)).reshape(-1)
    wet_count = jnp.sum(wet_cells)
    grid_rows = jnp.arange(ROWS, dtype=jnp.int32)[:, None]
    grid_cols = jnp.arange(COLS, dtype=jnp.int32)[None, :]
    spread = jnp.float32(MEMBERS - 1)
    loc_radius = float(LOC_RADIUS)
    for batch_num in range(BATCHES):
        obs_slot = obs_index[batch_num]
        owner_dev = obs_owner[batch_num]
        obs_rows = owner_dev // N_DOMAIN * ROWS_DEV + obs_slot[:, 2]
        obs_cols = owner_dev % N_DOMAIN * COLS_DEV + obs_slot[:, 3]
        level_of = obs_slot[:, 0] * LEVELS + obs_slot[:, 1]
        position = (level_of * ROWS + obs_rows) * COLS + obs_cols
        priors = jnp.take(flat_state, position.astype(jnp.int32), axis=1).T
        mutual = gaspari(separation(obs_rows[:, None], obs_cols[:, None], obs_rows[None, :], obs_cols[None, :], COLS), loc_radius)
        before = flat_state
        for obs_num in range(OBS_BATCH):
            prior_row = priors[obs_num]
            mean_prior = jnp.mean(prior_row)
            anomaly = prior_row - mean_prior
            obs_var = obs_error[batch_num, obs_num]
            denominator = jnp.sum(anomaly * anomaly) / spread + obs_var
            shrink = 1.0 / (1.0 + jnp.sqrt(obs_var / denominator))
            weight = obs_value[batch_num, obs_num] - mean_prior - shrink * anomaly
            taper = gaspari(separation(grid_rows, grid_cols, obs_rows[obs_num], obs_cols[obs_num], COLS), loc_radius)
            taper_flat = jnp.broadcast_to(taper[None], (levels_total, ROWS, COLS)).reshape(-1) * wet_flat
            covariance = jnp.dot(anomaly, flat_state, precision=lax.Precision.HIGHEST)
            kalman = taper_flat * covariance / (spread * denominator)
            flat_state = flat_state + weight[:, None] * kalman[None, :]
            prior_cov = jnp.dot(priors, anomaly, precision=lax.Precision.HIGHEST)
            priors = priors + (mutual[obs_num] * prior_cov / (spread * denominator))[:, None] * weight[None, :]
        change = lax.optimization_barrier(jnp.sum((flat_state - before).reshape(MEMBERS, levels_total, -1), axis=0))
        total_inc = lax.optimization_barrier(jnp.sum(change * wet_cells[None, :], axis=1))
        offset = total_inc / (MEMBERS * wet_count)
        flat_state = (flat_state.reshape(MEMBERS, levels_total, -1) - offset[None, :, None] * wet_cells[None, None, :]).reshape(MEMBERS, -1)
    return flat_state.reshape(MEMBERS, FIELDS, LEVELS, ROWS, COLS)
```

```python
import functools

import jax
import jax.numpy as jnp
from jax import lax
from jax.experimental import pallas as pl
from jax.experimental.pallas import tpu as pltpu
from jax.sharding import PartitionSpec as P

LOC_RADIUS = 64
LANES = 128
SUBS = 8
F32 = jnp.float32
BF16 = jnp.bfloat16
HIGHEST = lax.Precision.HIGHEST
VMEM = pltpu.VMEM
SMEM = pltpu.SMEM


def gaspari(scaled):
    scaled_safe = jnp.maximum(scaled, 1.0)
    near_part = (
        ((-0.25 * scaled + 0.5) * scaled + 0.625) * scaled - 5.0 / 3.0
    ) * scaled * scaled + 1.0
    far_part = (
        ((((scaled / 12.0 - 0.5) * scaled + 0.625) * scaled + 5.0 / 3.0) * scaled - 5.0) * scaled
        + 4.0
        - 2.0 / (3.0 * scaled_safe)
    )
    return jnp.where(scaled <= 1.0, near_part, jnp.where(scaled < 2.0, far_part, 0.0))


def taper(row_gap, col_gap, grid_width):
    col_gap = jnp.abs(col_gap)
    col_gap = jnp.minimum(col_gap, grid_width - col_gap)
    square = (col_gap * col_gap + row_gap * row_gap).astype(F32)
    return gaspari(jnp.sqrt(square) * (1.0 / LOC_RADIUS))


def iota(shape, dim):
    return lax.broadcasted_iota(jnp.int32, shape, dim)


def split(value):
    high = value.astype(BF16)
    return high, (value - high.astype(F32)).astype(BF16)


def dot(a, b):
    return lax.dot_general(a, b, (((1,), (0,)), ((), ())), preferred_element_type=F32)


def dot_exact(a, b, dims):
    return lax.dot_general(
        a, b, ((dims[:1], dims[1:]), ((), ())), precision=HIGHEST, preferred_element_type=F32
    )


class Sizes:
    def __init__(self, ensemble, velocity, obs_index):
        self.own, self.fields, self.levels, self.rows, self.cols = ensemble.shape
        self.states = self.fields * self.levels
        self.groups_m = lax.axis_size("member")
        self.groups_d = lax.axis_size("domain")
        self.members = self.own * self.groups_m
        self.block_rows = self.rows // self.groups_m
        self.col_tiles = self.cols // LANES
        self.cells = self.block_rows * self.col_tiles
        self.per_step = SUBS // self.cells
        self.steps = self.states // self.per_step
        self.width = self.cols * self.groups_d
        self.batches, self.batch = obs_index.shape[:2]
        self.obs = self.batches * self.batch
        self.halo = -(-self.own * self.states // LANES) * LANES
        self.packs = -(-self.own // SUBS)
        self.pack_states = LANES // self.obs
        self.sum_rows = -(-self.states // self.pack_states)


def edges_kernel(z, x_ref, first_ref, last_ref):
    step = pl.program_id(0)

    @pl.when(step == 0)
    def _():
        first_ref[...] = jnp.zeros_like(first_ref)
        last_ref[...] = jnp.zeros_like(last_ref)

    lane = iota((z.rows, z.halo), 1)
    first, last = first_ref[...], last_ref[...]
    for q in range(z.per_step):
        base = (step * z.per_step + q) * z.own
        for m in range(z.own):
            hit = lane == base + m
            first = jnp.where(hit, x_ref[m, q, :, 0:1], first)
            last = jnp.where(hit, x_ref[m, q, :, z.cols - 1 : z.cols], last)
    first_ref[...] = first
    last_ref[...] = last


def forecast_kernel(
    z, place, index, owner, diff, x_ref, before_ref, after_ref, vel_ref, mask_ref, out_ref, obs_ref,
    state, picked, sems,
):
    step = pl.program_id(0)
    shape = (z.rows, z.cols)
    row, col = iota(shape, 0), iota(shape, 1)
    wet = mask_ref[...].astype(F32)
    stride = z.states * z.cells
    flat = state.reshape(z.members * stride, LANES)
    for q in range(z.per_step):
        fl = step * z.per_step + q
        level = lax.rem(fl, z.levels)
        spread = diff[fl // z.levels]
        half_u = 0.5 * vel_ref[0, level]
        half_v = 0.5 * vel_ref[1, level]
        center = wet * (1.0 - 4.0 * spread)
        east = wet * (spread - half_u)
        west = wet * (spread + half_u)
        north = jnp.where(row == z.rows - 1, 0.0, wet * (spread - half_v))
        south = jnp.where(row == 0, 0.0, wet * (spread + half_v))
        turn = lax.rem(z.halo - fl * z.own, z.halo)
        before = pltpu.roll(before_ref[...], turn, 1)
        after = pltpu.roll(after_ref[...], turn, 1)
        for m in range(z.own):
            x = x_ref[m, q]
            nxt = jnp.where(col == z.cols - 1, after[:, m : m + 1], pltpu.roll(x, z.cols - 1, 1))
            prv = jnp.where(col == 0, before[:, m : m + 1], pltpu.roll(x, 1, 1))
            y = (
                center * x
                + east * nxt
                + west * prv
                + north * pltpu.roll(x, z.rows - 1, 0)
                + south * pltpu.roll(x, 1, 0)
            )
            for p in range(z.groups_m):
                for c in range(z.col_tiles):
                    at = (p * z.own + m) * stride + q * z.cells + c * z.block_rows
                    flat[pl.ds(pl.multiple_of(step * SUBS, SUBS) + at, z.block_rows), :] = y[
                        p * z.block_rows : (p + 1) * z.block_rows, c * LANES : (c + 1) * LANES
                    ]

    def copy(at):
        lines = pl.ds(pl.multiple_of(at * SUBS, SUBS), SUBS)
        return pltpu.make_async_copy(state.at[:, lines, :], out_ref.at[:, lines, :], sems.at[at])

    copy(step).start()

    @pl.when(step == z.steps - 1)
    def _():
        picked[...] = jnp.zeros_like(picked)
        lane = iota((z.own, LANES), 1)

        def pick(k, carry):
            b, i = k // z.batch, lax.rem(k, z.batch)

            @pl.when(lax.rem(owner[b], z.groups_d) == place[1])
            def _():
                fl = index[b, i, 0] * z.levels + index[b, i, 1]
                at = index[b, i, 3]
                cell = (at // LANES) * z.block_rows + index[b, i, 2]
                base = (owner[b] // z.groups_d) * z.own * stride + fl * z.cells + cell
                got = flat[pl.ds(base, z.own, stride=stride), :]
                got = jnp.sum(
                    jnp.where(lane == lax.rem(at, LANES), got, 0.0), axis=1, keepdims=True
                )
                picked[0 : z.own, :] = jnp.where(lane == k, got, picked[0 : z.own, :])

            return carry

        lax.fori_loop(0, z.obs, pick, 0)
        total = picked[0:SUBS, :]
        for v in range(1, z.packs):
            total = total + pltpu.roll(picked[v * SUBS : (v + 1) * SUBS, :], v * z.obs, 1)
        obs_ref[...] = total

        def drain(i, carry):
            copy(i).wait()
            return carry

        lax.fori_loop(0, z.steps, drain, 0)


def filter_kernel(
    z, place, index, owner, value, error, got_ref, mask_ref,
    gain_ref, cross_ref, lift_ref, taper_ref, relay_ref, gap_ref, wet_ref,
):
    n = z.obs
    eight = z.groups_m * SUBS
    stacked = []
    for s in range(z.groups_m):
        total = got_ref[s * z.groups_d]
        for d in range(1, z.groups_d):
            total = total + got_ref[s * z.groups_d + d]
        stacked.append(total)
    stacked = jnp.concatenate(stacked, axis=0)
    square = (n, LANES)
    prior = jnp.zeros(square, F32)
    row, lane = iota(square, 0), iota(square, 1)
    for v in range(z.packs):
        pick = (lane == row + v * n).astype(F32)
        part = dot_exact(pick, stacked, (1, 1))
        src = iota((eight, LANES), 0)
        dst = iota((eight, LANES), 1)
        slot = v * SUBS + src % SUBS
        place_of = jnp.where(slot < z.own, (src // SUBS) * z.own + slot, -1)
        prior = prior + dot_exact(part, (dst == place_of).astype(F32), (1, 0))
    ones = jnp.full((SUBS, LANES), 1.0 / z.members, F32)
    mean_row = dot_exact(ones, prior, (1, 1))
    mean = jnp.sum(prior, axis=1, keepdims=True) * (1.0 / z.members)
    anomaly = jnp.where(lane < z.members, prior - mean, 0.0)
    rows_s, cols_s = jnp.zeros(square, jnp.int32), jnp.zeros(square, jnp.int32)
    rows_l, cols_l = rows_s, cols_s
    values = jnp.zeros((SUBS, n), F32)
    value_lane = iota((SUBS, n), 1)
    shape = (SUBS, LANES)
    sub = iota(shape, 0) % z.cells
    tile_col = (sub // z.block_rows) * LANES + iota(shape, 1)
    cell_row = place[0] * z.block_rows + sub % z.block_rows
    cell_col = place[1] * z.cols + tile_col
    wet = jnp.zeros(shape, F32)
    line_of = iota(shape, 0) + place[0] * SUBS
    for c in range(z.col_tiles):
        for full_row in range(z.rows):
            line = mask_ref[full_row : full_row + 1, c * LANES : (c + 1) * LANES].astype(F32)
            p, r = divmod(full_row, z.block_rows)
            for q in range(z.per_step):
                spot = p * SUBS + q * z.cells + c * z.block_rows + r
                wet = jnp.where(line_of == spot, line, wet)
    wet_ref[...] = wet
    for k in range(n):
        b, i = divmod(k, z.batch)
        at_row = owner[b] // z.groups_d * z.block_rows + index[b, i, 2]
        at_col = lax.rem(owner[b], z.groups_d) * z.cols + index[b, i, 3]
        rows_s = jnp.where(row == k, at_row, rows_s)
        cols_s = jnp.where(row == k, at_col, cols_s)
        rows_l = jnp.where(lane == k, at_row, rows_l)
        cols_l = jnp.where(lane == k, at_col, cols_l)
        values = jnp.where(value_lane == k, value[b, i], values)
        taper_ref[k] = wet * taper(cell_row - at_row, cell_col - at_col, z.width)
    gap_ref[...] = jnp.zeros_like(gap_ref)
    gap_ref[:, 0:n] = values - mean_row
    mutual = taper(rows_s - rows_l, cols_s - cols_l, z.width)
    relay = jnp.zeros(square, F32)
    inverse_l = jnp.zeros(square, F32)
    inverse_s = jnp.zeros(square, F32)
    shrink_s = jnp.zeros(square, F32)
    spread = float(z.members - 1)
    for k in range(n):
        b, i = divmod(k, z.batch)
        own = anomaly[k : k + 1, :]
        product = jnp.sum(anomaly * own, axis=1, keepdims=True)
        variance = product[k : k + 1, :] * (1.0 / spread) + error[b, i]
        inverse = 1.0 / (spread * variance)
        shrink = 1.0 / (1.0 + jnp.sqrt(error[b, i] / variance))
        ratio = jnp.where(row[:, 0:1] > k, mutual[:, k : k + 1] * product * inverse, 0.0)
        anomaly = anomaly - (shrink * ratio) * own
        relay = jnp.where(lane == k, ratio, relay)
        inverse_l = jnp.where(lane == k, inverse, inverse_l)
        inverse_s = jnp.where(row == k, inverse, inverse_s)
        shrink_s = jnp.where(row == k, shrink, shrink_s)
    gram = dot_exact(anomaly, anomaly, (1, 1))
    cross_ref[...] = -shrink_s[:, 0:n] * inverse_l[:, 0:n] * gram
    high, low = split(anomaly * inverse_s)
    gain_ref[0:n, :] = high[:, 0 : z.members]
    gain_ref[n : 2 * n, :] = low[:, 0 : z.members]
    eye = (iota((z.members, LANES), 0) == iota((z.members, LANES), 1)).astype(F32)
    lift_ref[...] = dot_exact(eye, shrink_s * anomaly, (1, 1))
    eye = (iota((n, LANES), 0) == iota((n, LANES), 1)).astype(F32)
    relay_ref[...] = dot_exact(eye, relay, (1, 1))


def gain_kernel(z, cross, x_ref, gain_ref, taper_ref, wet_ref, kalman_ref, sums_ref, work, held):
    n = z.obs
    step = pl.program_id(0)
    flat_x = x_ref.reshape(z.members * SUBS, LANES)
    flat_k = kalman_ref.reshape(SUBS * n, LANES)
    both = gain_ref[...]
    high = gain_ref[0:n, :]
    for s in range(0, SUBS, 2):
        x = jnp.concatenate(
            [flat_x[pl.ds(s + t, z.members, stride=SUBS), :] for t in range(2)], axis=1
        )
        x_high, x_low = split(x)
        first = dot(both, x_high)
        total = first[0:n] + first[n : 2 * n] + dot(high, x_low)
        work[s * n : (s + 1) * n, :] = total[:, 0:LANES]
        work[(s + 1) * n : (s + 2) * n, :] = total[:, LANES : 2 * LANES]
    part = [work[pl.ds(k, SUBS, stride=n), :] for k in range(n)]
    for k in range(n):
        kalman = taper_ref[k] * part[k]
        flat_k[pl.ds(k, SUBS, stride=n), :] = kalman
        for j in range(k + 1, n):
            part[j] = part[j] + cross[k, j] * kalman
    for q in range(z.per_step):
        total = flat_k[q * z.cells * n : (q * z.cells + 1) * n, :]
        for s in range(q * z.cells + 1, (q + 1) * z.cells):
            total = total + flat_k[s * n : (s + 1) * n, :]
        at = pl.multiple_of((step * z.per_step + q) * n, n)
        held[pl.ds(at, n), :] = total

    @pl.when(step == z.steps - 1)
    def _():
        ones = jnp.ones((SUBS, LANES), F32)
        sums_ref[...] = jnp.zeros_like(sums_ref)
        for i in range(z.sum_rows):
            line = dot_exact(ones, held[i * LANES : (i + 1) * LANES, :], (1, 1))
            sums_ref[i : i + 1, :] = line[0:1, :]
        wet = jnp.sum(wet_ref[0 : z.cells, :], axis=0, keepdims=True)
        sums_ref[z.sum_rows : z.sum_rows + 1, :] = wet


def update_kernel(
    z, index, x_ref, kalman_ref, sums_ref, lift_ref, relay_ref, gap_ref, wet_ref, out_ref,
    weight, moved,
):
    n = z.obs
    step = pl.program_id(0)

    @pl.when(step == 0)
    def _():
        sums = sums_ref[0]
        for d in range(1, z.groups_m * z.groups_d):
            sums = sums + sums_ref[d]
        count = jnp.sum(sums[z.sum_rows : z.sum_rows + 1, :], axis=1, keepdims=True)
        lines = []
        for fl in range(z.states):
            i, c = divmod(fl, z.pack_states)
            lines.append(sums[i : i + 1, c * n : (c + 1) * n])
        pad = -z.states % SUBS
        table = jnp.concatenate(lines + [jnp.zeros((pad, n), F32)], axis=0) / count
        eye = (iota((n, n), 0) == iota((n, n), 1)).astype(F32)
        turned = dot_exact(eye, table, (1, 1))
        shape = (z.states + pad, n)
        fl_row, lane = iota(shape, 0), iota(shape, 1)
        at = jnp.zeros(shape, jnp.int32)
        for k in range(n):
            b, i = divmod(k, z.batch)
            at = jnp.where(lane == k, index[b, i, 0] * z.levels + index[b, i, 1], at)
        chosen = dot_exact(turned, (fl_row == at).astype(F32), (1, 0))
        later = iota((n, n), 1) // z.batch > iota((n, n), 0) // z.batch
        relay = relay_ref[...] - jnp.where(later, chosen, 0.0)
        gap = gap_ref[0:1, 0:n]
        for k in range(n):
            gap = gap - gap[:, k : k + 1] * relay[k : k + 1, :]
        shift = jnp.sum(table * gap, axis=1, keepdims=True)
        moved[...] = jnp.broadcast_to(shift, moved.shape)
        high, low = split(gap - lift_ref[...])
        weight[0 : z.members, :] = high
        weight[z.members : 2 * z.members, :] = low

    flat_x = x_ref.reshape(z.members * SUBS, LANES)
    flat_o = out_ref.reshape(z.members * SUBS, LANES)
    both = weight[...]
    high = weight[0 : z.members, :]
    for s in range(0, SUBS, 2):
        k_high, k_low = split(jnp.concatenate([kalman_ref[0, s], kalman_ref[0, s + 1]], axis=1))
        first = dot(both, k_high)
        total = first[0 : z.members] + first[z.members : 2 * z.members] + dot(high, k_low)
        for t in range(2):
            fl = step * z.per_step + (s + t) // z.cells
            off = moved[pl.ds(fl, 1), :] * wet_ref[s + t : s + t + 1, :]
            old = flat_x[pl.ds(s + t, z.members, stride=SUBS), :]
            flat_o[pl.ds(s + t, z.members, stride=SUBS), :] = (
                old + total[:, t * LANES : (t + 1) * LANES] - off
            )


def whole(*shape):
    return pl.BlockSpec(shape, lambda *_: (0,) * len(shape))


def smem():
    return pl.BlockSpec(memory_space=SMEM)


def struct(*shape, dtype=F32):
    return jax.ShapeDtypeStruct(shape, dtype)


def spread_out(tile, axes):
    count = lax.axis_size(axes)
    copies = jnp.broadcast_to(tile[None], (count,) + tile.shape)
    return lax.all_to_all(copies, axes, 0, 0, tiled=True)


def local(ensemble, velocity, diffusivity, land_mask, obs_index, obs_owner, obs_value, obs_error):
    z = Sizes(ensemble, velocity, obs_index)
    axes = ("member", "domain")
    place = jnp.stack([lax.axis_index("member"), lax.axis_index("domain")]).astype(jnp.int32)
    state = ensemble.reshape(z.own, z.states, z.rows, z.cols)
    slab = pl.BlockSpec((z.own, z.per_step, z.rows, z.cols), lambda i: (0, i, 0, 0))
    first, last = pl.pallas_call(
        functools.partial(edges_kernel, z),
        grid=(z.steps,),
        in_specs=[slab],
        out_specs=[whole(z.rows, z.halo)] * 2,
        out_shape=[struct(z.rows, z.halo)] * 2,
        name="edges",
    )(state)
    up = [(i, (i + 1) % z.groups_d) for i in range(z.groups_d)]
    down = [(j, i) for i, j in up]
    before = lax.ppermute(last, "domain", up)
    after = lax.ppermute(first, "domain", down)
    lines = z.states * z.cells
    stepped, own_priors = pl.pallas_call(
        functools.partial(forecast_kernel, z),
        grid=(z.steps,),
        in_specs=[
            smem(),
            smem(),
            smem(),
            smem(),
            slab,
            whole(z.rows, z.halo),
            whole(z.rows, z.halo),
            whole(*velocity.shape),
            whole(*land_mask.shape),
        ],
        out_specs=[pl.BlockSpec(memory_space=pl.ANY), whole(SUBS, LANES)],
        out_shape=[struct(z.members, lines, LANES), struct(SUBS, LANES)],
        scratch_shapes=[
            VMEM((z.members, lines, LANES), F32),
            VMEM((z.packs * SUBS, LANES), F32),
            pltpu.SemaphoreType.DMA((z.steps,)),
        ],
        name="forecast",
    )(place, obs_index, obs_owner, diffusivity, state, before, after, velocity, land_mask)
    current = lax.all_to_all(stepped, "member", 0, 0, tiled=True)
    priors = spread_out(own_priors, axes)
    n = z.obs
    vmem = pl.BlockSpec(memory_space=VMEM)
    gain, cross, lift, tapers, relay, gap, wet = pl.pallas_call(
        functools.partial(filter_kernel, z),
        in_specs=[smem()] * 5 + [vmem, vmem],
        out_specs=[vmem] * 7,
        out_shape=[
            struct(2 * n, z.members, dtype=BF16),
            struct(n, n),
            struct(z.members, n),
            struct(n, SUBS, LANES),
            struct(n, n),
            struct(SUBS, LANES),
            struct(SUBS, LANES),
        ],
        name="filter",
    )(place, obs_index, obs_owner, obs_value, obs_error, priors, land_mask)
    column = pl.BlockSpec((z.members, SUBS, LANES), lambda i: (0, i, 0))
    kalman_spec = pl.BlockSpec((1, SUBS, n, LANES), lambda i: (i, 0, 0, 0))
    kalman, sums = pl.pallas_call(
        functools.partial(gain_kernel, z),
        grid=(z.steps,),
        in_specs=[
            smem(),
            column,
            whole(2 * n, z.members),
            whole(n, SUBS, LANES),
            whole(SUBS, LANES),
        ],
        out_specs=[kalman_spec, whole(z.sum_rows + 1, LANES)],
        out_shape=[struct(z.steps, SUBS, n, LANES), struct(z.sum_rows + 1, LANES)],
        scratch_shapes=[VMEM((SUBS * n, LANES), F32), VMEM((z.sum_rows * LANES, LANES), F32)],
        name="gain",
    )(cross, current, gain, tapers, wet)
    sums = spread_out(sums, axes)
    padded = z.states + -z.states % SUBS
    result = pl.pallas_call(
        functools.partial(update_kernel, z),
        grid=(z.steps,),
        in_specs=[
            smem(),
            column,
            kalman_spec,
            whole(*sums.shape),
            whole(z.members, n),
            whole(n, n),
            whole(SUBS, LANES),
            whole(SUBS, LANES),
        ],
        out_specs=column,
        out_shape=struct(z.members, lines, LANES),
        scratch_shapes=[VMEM((2 * z.members, n), BF16), VMEM((padded, LANES), F32)],
        name="update",
    )(obs_index, current, kalman, sums, lift, relay, gap, wet)
    result = result.reshape(z.members, z.fields, z.levels, z.col_tiles, z.block_rows, LANES)
    result = jnp.swapaxes(result, 3, 4)
    return result.reshape(z.members, z.fields, z.levels, z.block_rows, z.cols)


def solution(mesh):
    in_specs = (
        P("member", None, None, None, "domain"),
        P(None, None, None, "domain"),
        P(),
        P(None, "domain"),
        P(),
        P(),
        P(),
        P(),
    )
    out_specs = P(None, None, None, "member", "domain")
    return jax.shard_map(local, mesh=mesh, in_specs=in_specs, out_specs=out_specs, check_vma=False)
```

```python
import functools

import jax
import jax.numpy as jnp
from jax import lax
from jax.experimental import pallas as pl
from jax.experimental.pallas import tpu as pltpu
from jax.sharding import PartitionSpec as P


LOC_RADIUS = 64
LANES = 128
SUBS = 8
F32 = jnp.float32
BF16 = jnp.bfloat16
HIGHEST = lax.Precision.HIGHEST
VMEM = pltpu.VMEM
SMEM = pltpu.SMEM


def gaspari(scaled):
    scaled_safe = jnp.maximum(scaled, 1.0)
    near_part = (
        ((-0.25 * scaled + 0.5) * scaled + 0.625) * scaled - 5.0 / 3.0
    ) * scaled * scaled + 1.0
    far_part = (
        ((((scaled / 12.0 - 0.5) * scaled + 0.625) * scaled + 5.0 / 3.0) * scaled - 5.0) * scaled
        + 4.0
        - 2.0 / (3.0 * scaled_safe)
    )
    return jnp.where(scaled <= 1.0, near_part, jnp.where(scaled < 2.0, far_part, 0.0))


def taper(row_gap, col_gap, grid_width):
    col_gap = jnp.abs(col_gap)
    col_gap = jnp.minimum(col_gap, grid_width - col_gap)
    square = (col_gap * col_gap + row_gap * row_gap).astype(F32)
    return gaspari(jnp.sqrt(square) * (1.0 / LOC_RADIUS))


def iota(shape, dim):
    return lax.broadcasted_iota(jnp.int32, shape, dim)


def split(value):
    high = value.astype(BF16)
    return high, (value - high.astype(F32)).astype(BF16)


def dot(a, b):
    return lax.dot_general(a, b, (((1,), (0,)), ((), ())), preferred_element_type=F32)


def dot_exact(a, b, dims):
    return lax.dot_general(
        a, b, ((dims[:1], dims[1:]), ((), ())), precision=HIGHEST, preferred_element_type=F32
    )


class Sizes:
    def __init__(self, ensemble, obs_index):
        self.own, self.fields, self.levels, self.rows, self.cols = ensemble.shape
        self.states = self.fields * self.levels
        self.groups_m = lax.axis_size("member")
        self.groups_d = lax.axis_size("domain")
        self.members = self.own * self.groups_m
        self.block_rows = self.rows // self.groups_m
        self.col_tiles = self.cols // LANES
        self.cells = self.block_rows * self.col_tiles
        self.per_step = SUBS // self.cells
        self.steps = self.states // self.per_step
        self.width = self.cols * self.groups_d
        self.batches, self.batch = obs_index.shape[:2]
        self.obs = self.batches * self.batch
        self.pack_states = LANES // self.obs
        self.sum_rows = -(-self.states // self.pack_states)
        self.part = next(m for m in (5, 4, 3, 2, 1) if self.own % m == 0)
        self.parts = self.own // self.part
        self.lines = self.states * self.cells
        self.groups = next(g for g in (3, 2, 1) if self.steps % g == 0)
        self.window = -(-self.own // SUBS) * SUBS

    def start(self, p):
        return min(p * self.own, self.members - self.window)


def arrivals(z, step, source, held, sems):
    def copy(at):
        part = pl.ds(at * z.part, z.part)
        return pltpu.make_async_copy(source.at[part], held.at[part], sems.at[at])

    @pl.when(step == 0)
    def _():
        for at in range(z.parts):
            copy(at).start()

    copy(step).wait()


def edges_kernel(z, source, first_ref, last_ref, held, sems):
    step = pl.program_id(0)
    arrivals(z, step, source, held, sems)
    lane = iota((z.rows, LANES), 1)
    first = jnp.zeros((z.rows, LANES), F32)
    last = first
    for m in range(z.part):
        for fl in range(z.states):
            hit = lane == m * z.states + fl
            at = step * z.part + m
            first = jnp.where(hit, held[at, fl, :, 0:1], first)
            last = jnp.where(hit, held[at, fl, :, z.cols - 1 : z.cols], last)
    first_ref[...] = first
    last_ref[...] = last


def forecast_kernel(
    z, group, domain, index, owner, diff, source, before_ref, after_ref, vel_ref, mask_ref,
    out_ref, *refs,
):
    others = refs[: z.groups_m - 1]
    obs_ref, held, state, picked, in_sems, sems = refs[z.groups_m - 1 :]
    step = pl.program_id(0)
    arrivals(z, step, source, held, in_sems)
    shape = (z.rows, z.cols)
    row, col = iota(shape, 0), iota(shape, 1)
    wet = mask_ref[...].astype(F32)
    flat = state.reshape(z.members * z.lines, LANES)
    member = pl.multiple_of(step * (z.part * z.lines), SUBS)
    side = pl.ds(pl.multiple_of(step * LANES, LANES), LANES)
    before = before_ref[:, side]
    after = after_ref[:, side]
    for fl in range(z.states):
        level = fl % z.levels
        spread = diff[fl // z.levels]
        half_u = 0.5 * vel_ref[0, level]
        half_v = 0.5 * vel_ref[1, level]
        center = wet * (1.0 - 4.0 * spread)
        east = wet * (spread - half_u)
        west = wet * (spread + half_u)
        north = jnp.where(row == z.rows - 1, 0.0, wet * (spread - half_v))
        south = jnp.where(row == 0, 0.0, wet * (spread + half_v))
        for m in range(z.part):
            x = held[step * z.part + m, fl]
            at = m * z.states + fl
            nxt = jnp.where(col == z.cols - 1, after[:, at : at + 1], pltpu.roll(x, z.cols - 1, 1))
            prv = jnp.where(col == 0, before[:, at : at + 1], pltpu.roll(x, 1, 1))
            y = (
                center * x
                + east * nxt
                + west * prv
                + north * pltpu.roll(x, z.rows - 1, 0)
                + south * pltpu.roll(x, 1, 0)
            )
            for p in range(z.groups_m):
                for c in range(z.col_tiles):
                    line = (p * z.own + m) * z.lines + fl * z.cells + c * z.block_rows
                    flat[pl.ds(member + line, z.block_rows), :] = y[
                        p * z.block_rows : (p + 1) * z.block_rows, c * LANES : (c + 1) * LANES
                    ]

    def copies(at):
        part = pl.ds(at * z.part, z.part)
        yield pltpu.make_async_copy(state.at[:, part], out_ref.at[:, part], sems.at[0, at])
        for x, other in enumerate(others, 1):
            p = jnp.bitwise_xor(group[0], x)
            yield pltpu.make_async_copy(state.at[p, part], other.at[part], sems.at[x, at])

    for copy in copies(step):
        copy.start()

    @pl.when(step == z.parts - 1)
    def _():
        picked[...] = jnp.zeros_like(picked)
        lane = iota((z.own, LANES), 1)

        def pick(k, carry):
            b, i = k // z.batch, lax.rem(k, z.batch)

            @pl.when(lax.rem(owner[b], z.groups_d) == domain[0])
            def _():
                fl = index[b, 0, i] * z.levels + index[b, 1, i]
                at = index[b, 3, i]
                cell = (at // LANES) * z.block_rows + index[b, 2, i]
                base = (owner[b] // z.groups_d) * z.own * z.lines + fl * z.cells + cell
                got = flat[pl.ds(base, z.own, stride=z.lines), :]
                got = jnp.where(lane == lax.rem(at, LANES), got, 0.0)
                got = jnp.sum(got, axis=1, keepdims=True)
                picked[0 : z.own, :] = jnp.where(lane == k, got, picked[0 : z.own, :])

            return carry

        lax.fori_loop(0, z.obs, pick, 0)
        total = picked[0:SUBS, :]
        for v in range(1, z.window // SUBS):
            total = total + pltpu.roll(picked[v * SUBS : (v + 1) * SUBS, :], v * z.obs, 1)
        obs_ref[...] = total

        def drain(at, carry):
            for copy in copies(at):
                copy.wait()
            return carry

        lax.fori_loop(0, z.parts, drain, 0)


def filter_kernel(
    z, domain, index, owner, value, error, got_ref, mask_ref,
    gain_ref, part_ref, cross_ref, flag, lift_ref, taper_ref, relay_ref, gap_ref, wet_ref,
):
    n = z.obs
    eight = z.groups_m * SUBS
    stacked = []
    for x in range(z.groups_m):
        total = got_ref[0, x]
        for d in range(1, z.groups_d):
            total = total + got_ref[d, x]
        stacked.append(total)
    stacked = jnp.concatenate(stacked, axis=0)
    square = (n, LANES)
    prior = jnp.zeros(square, F32)
    row, lane = iota(square, 0), iota(square, 1)
    for v in range(z.window // SUBS):
        pick = (lane == row + v * n).astype(F32)
        part = dot_exact(pick, stacked, (1, 1))
        src = iota((eight, LANES), 0)
        dst = iota((eight, LANES), 1)
        slot = v * SUBS + src % SUBS
        place_of = jnp.where(slot < z.own, (src // SUBS) * z.own + slot, -1)
        prior = prior + dot_exact(part, (dst == place_of).astype(F32), (1, 0))
    ones = jnp.full((SUBS, LANES), 1.0 / z.members, F32)
    mean_row = dot_exact(ones, prior, (1, 1))
    mean = jnp.sum(prior, axis=1, keepdims=True) * (1.0 / z.members)
    anomaly = jnp.where(lane < z.members, prior - mean, 0.0)
    rows_s, cols_s = jnp.zeros(square, jnp.int32), jnp.zeros(square, jnp.int32)
    rows_l, cols_l = rows_s, cols_s
    values = jnp.zeros((SUBS, n), F32)
    value_lane = iota((SUBS, n), 1)
    shape = (SUBS, LANES)
    sub = iota(shape, 0) % z.cells
    cell_row = sub % z.block_rows
    first_col = domain[0] * z.cols
    cell_col = first_col + (sub // z.block_rows) * LANES + iota(shape, 1)
    wets = []
    for p in range(z.groups_m):
        wet = jnp.zeros(shape, F32)
        for c in range(z.col_tiles):
            for r in range(z.block_rows):
                full_row = p * z.block_rows + r
                line = mask_ref[full_row : full_row + 1, c * LANES : (c + 1) * LANES]
                wet = jnp.where(sub == c * z.block_rows + r, line.astype(F32), wet)
        wet_ref[p] = wet
        wets.append(wet)
    for b in range(z.batches):
        near = jnp.int32(0)
        tile = lax.rem(owner[b], z.groups_d) * z.cols
        first_row = owner[b] // z.groups_d * z.block_rows
        for i in range(z.batch):
            k = b * z.batch + i
            at_row = first_row + index[b, 2, i]
            at_col = tile + index[b, 3, i]
            rows_s = jnp.where(row == k, at_row, rows_s)
            cols_s = jnp.where(row == k, at_col, cols_s)
            rows_l = jnp.where(lane == k, at_row, rows_l)
            cols_l = jnp.where(lane == k, at_col, cols_l)
            values = jnp.where(value_lane == k, value[b, i], values)
            ahead = lax.rem(at_col - first_col + z.width, z.width)
            behind = z.width - ahead
            reach = 2 * LOC_RADIUS
            close = (ahead < z.cols + reach) | (behind < reach)
            near = jnp.where(close, 1, near)
        flag[b] = near

        @pl.when(near > 0)
        def _():
            for i in range(z.batch):
                k = b * z.batch + i
                at_row = first_row + index[b, 2, i]
                at_col = tile + index[b, 3, i]
                for p in range(z.groups_m):
                    rho = taper(cell_row + (p * z.block_rows - at_row), cell_col - at_col, z.width)
                    taper_ref[p, k] = wets[p] * rho

    gap_ref[...] = jnp.zeros_like(gap_ref)
    gap_ref[:, 0:n] = values - mean_row
    mutual = taper(rows_s - rows_l, cols_s - cols_l, z.width)
    relay = jnp.zeros(square, F32)
    inverse_l = jnp.zeros(square, F32)
    inverse_s = jnp.zeros(square, F32)
    shrink_s = jnp.zeros(square, F32)
    spread = float(z.members - 1)
    for k in range(n):
        b, i = divmod(k, z.batch)
        own = anomaly[k : k + 1, :]
        product = jnp.sum(anomaly * own, axis=1, keepdims=True)
        variance = product[k : k + 1, :] * (1.0 / spread) + error[b, i]
        inverse = 1.0 / (spread * variance)
        shrink = 1.0 / (1.0 + jnp.sqrt(error[b, i] / variance))
        ratio = jnp.where(row[:, 0:1] > k, mutual[:, k : k + 1] * product * inverse, 0.0)
        anomaly = anomaly - (shrink * ratio) * own
        relay = jnp.where(lane == k, ratio, relay)
        inverse_l = jnp.where(lane == k, inverse, inverse_l)
        inverse_s = jnp.where(row == k, inverse, inverse_s)
        shrink_s = jnp.where(row == k, shrink, shrink_s)
    gram = dot_exact(anomaly, anomaly, (1, 1))
    cross_ref[...] = -shrink_s[:, 0:n] * inverse_l[:, 0:n] * gram
    high, low = split(anomaly * inverse_s)

    def tripled(count, offset, width):
        shape = (LANES, 3 * width)
        src, dst = iota(shape, 0), iota(shape, 1)
        third, slot = dst // width, dst % width - offset
        hit = (src == slot) & (slot >= 0) & (slot < count)
        upper = (hit & (third < 2)).astype(BF16)
        lower = (hit & (third == 2)).astype(BF16)
        return (dot(high, upper) + dot(low, lower)).astype(BF16)

    gain_ref[...] = tripled(z.members, 0, z.members)
    made = {}
    for p in range(z.groups_m):
        offset = p * z.own - z.start(p)
        if offset not in made:
            made[offset] = tripled(z.own, offset, z.window)
        part_ref[p] = made[offset]
    eye = (iota((z.members, LANES), 0) == iota((z.members, LANES), 1)).astype(F32)
    lift_ref[...] = dot_exact(eye, shrink_s * anomaly, (1, 1))
    eye = (iota((n, LANES), 0) == iota((n, LANES), 1)).astype(F32)
    relay_ref[...] = dot_exact(eye, relay, (1, 1))


def stacked_rows(flat, first, count, lines):
    x = [flat[pl.ds(first + t, count, stride=lines), :] for t in range(2)]
    x = jnp.concatenate(x, axis=1)
    high = x.astype(BF16).astype(F32)
    return jnp.concatenate([high, x - high, high], axis=0).astype(BF16)


def solve_gains(z, flag, cross, taper_of, work, gains):
    n, size = z.obs, z.batch
    every = range(z.groups)

    for b in range(z.batches):

        @pl.when(flag[b] > 0)
        def _():
            part = [
                [work[pl.ds(g * SUBS * n + b * size + i, SUBS, stride=n), :] for g in every]
                for i in range(size)
            ]
            for before in range(b):

                def add(part):
                    part = [list(each) for each in part]
                    for j in range(before * size, (before + 1) * size):
                        held = [gains[g * n + j] for g in every]
                        for i in range(size):
                            factor = cross[j, b * size + i]
                            for g in every:
                                part[i][g] = part[i][g] + factor * held[g]
                    return part

                part = lax.cond(flag[before] > 0, add, lambda part: part, part)
            for i in range(size):
                k = b * size + i
                rho = taper_of(k)
                for g in every:
                    kalman = rho * part[i][g]
                    gains[g * n + k] = kalman
                    for j in range(i + 1, size):
                        part[j][g] = part[j][g] + cross[k, b * size + j] * kalman

        @pl.when(flag[b] == 0)
        def _():
            for i in range(size):
                for g in every:
                    gains[g * n + b * size + i] = jnp.zeros((SUBS, LANES), F32)


def sums_kernel(
    z, group, cross, flag, x_ref, part_ref, taper_ref, wet_ref, sums_ref, work, gains, total, held
):
    n = z.obs
    step = pl.program_id(0)
    lines = z.groups * SUBS
    flat = x_ref.reshape(z.members * lines, LANES)
    total[...] = jnp.zeros_like(total)
    every = range(z.groups)

    for p in range(z.groups_m):
        for g in every:
            for s in range(0, SUBS, 2):
                x = stacked_rows(flat, z.start(p) * lines + g * SUBS + s, z.window, lines)
                got = dot(part_ref[p], x)
                at = (g * SUBS + s) * n
                work[at : at + n, :] = got[:, 0:LANES]
                work[at + n : at + 2 * n, :] = got[:, LANES : 2 * LANES]
        solve_gains(z, flag, cross, lambda k: taper_ref[p, k], work, gains)
        for g in every:
            for k in range(n):
                total[g * n + k] = total[g * n + k] + gains[g * n + k]
    for g in every:
        for k in range(n):
            work[pl.ds(g * SUBS * n + k, SUBS, stride=n), :] = total[g * n + k]
        for q in range(z.per_step):
            first = g * SUBS + q * z.cells
            each = work[first * n : (first + 1) * n, :]
            for s in range(first + 1, first + z.cells):
                each = each + work[s * n : (s + 1) * n, :]
            fl = (step * z.groups + g) * z.per_step + q
            held[pl.ds(pl.multiple_of(fl * n, n), n), :] = each

    @pl.when(step == z.steps // z.groups - 1)
    def _():
        ones = jnp.ones((SUBS, LANES), F32)
        wet = jnp.sum(wet_ref[group[0]][0 : z.cells, :], axis=0, keepdims=True)
        rows = [
            dot_exact(ones, held[i * LANES : (i + 1) * LANES, :], (1, 1))[0:1, :]
            for i in range(z.sum_rows)
        ]
        rows.append(wet)
        for d in range(z.groups_d):
            for i, line in enumerate(rows):
                sums_ref[d, i : i + 1, :] = line


def weights_kernel(z, index, *refs):
    lift_ref, relay_ref, gap_ref, weight_ref, shift_ref = refs[z.groups_m :]
    n = z.obs
    sums = sum(ref[d] for ref in refs[: z.groups_m] for d in range(z.groups_d))
    count = jnp.sum(sums[z.sum_rows : z.sum_rows + 1, :], axis=1, keepdims=True)
    lines = []
    for fl in range(z.states):
        i, c = divmod(fl, z.pack_states)
        lines.append(sums[i : i + 1, c * n : (c + 1) * n])
    pad = -z.states % SUBS
    table = jnp.concatenate(lines + [jnp.zeros((pad, n), F32)], axis=0) / count
    eye = (iota((n, n), 0) == iota((n, n), 1)).astype(F32)
    turned = dot_exact(eye, table, (1, 1))
    shape = (z.states + pad, n)
    fl_row, lane = iota(shape, 0), iota(shape, 1)
    at = jnp.zeros(shape, jnp.int32)
    for k in range(n):
        b, i = divmod(k, z.batch)
        at = jnp.where(lane == k, index[b, 0, i] * z.levels + index[b, 1, i], at)
    chosen = dot_exact(turned, (fl_row == at).astype(F32), (1, 0))
    later = iota((n, n), 1) // z.batch > iota((n, n), 0) // z.batch
    relay = relay_ref[...] - jnp.where(later, chosen, 0.0)
    gap = gap_ref[0:1, 0:n]
    for k in range(n):
        gap = gap - gap[:, k : k + 1] * relay[k : k + 1, :]
    shift = jnp.sum(table * gap, axis=1, keepdims=True)
    shift_ref[...] = jnp.broadcast_to(shift, shift_ref.shape)
    high, low = split(gap - lift_ref[...])
    src, dst = iota((n, 3 * n), 0), iota((n, 3 * n), 1)
    hit = src == dst % n
    upper = (hit & (dst < 2 * n)).astype(BF16)
    lower = (hit & (dst >= 2 * n)).astype(BF16)
    weight_ref[...] = (dot(high, upper) + dot(low, lower)).astype(BF16)


def update_kernel(z, group, cross, flag, *refs):
    n = z.obs
    slabs = refs[: z.groups_m]
    gain_ref, taper_ref, wet_ref, weight_ref, shift_ref, out_ref = refs[z.groups_m : -6]
    got, made, work, gains, in_sems, out_sems = refs[-6:]
    chunk = z.groups * SUBS
    flat_x = got.reshape(z.members * z.lines, LANES)
    flat_o = made.reshape(z.members * z.lines, LANES)
    size = z.members * chunk
    every = range(z.groups)

    def lines(at):
        return pl.ds(pl.multiple_of(at * chunk, SUBS), chunk)

    def loads(at):
        for x, slab in enumerate(slabs):
            src = slab.at[group[0]] if x == 0 else slab
            here = got.at[at, x * z.own : (x + 1) * z.own]
            yield pltpu.make_async_copy(src.at[:, lines(at)], here, in_sems.at[x, at])

    def stores(at):
        for x in range(z.groups_m):
            first = jnp.bitwise_xor(group[0], x) * z.own
            here = made.at[at, x * z.own : (x + 1) * z.own]
            there = out_ref.at[pl.ds(first, z.own), lines(at)]
            yield pltpu.make_async_copy(here, there, out_sems.at[x, at])

    count = z.steps // z.groups
    for at in range(count):
        for copy in loads(at):
            copy.start()
    wet = wet_ref[group[0]]

    def advance(at, carry):
        for copy in loads(at):
            copy.wait()
        base = pl.multiple_of(at * size, SUBS)
        for g in every:
            for s in range(0, SUBS, 2):
                x = stacked_rows(flat_x, base + g * SUBS + s, z.members, chunk)
                new = dot(gain_ref[...], x)
                line = (g * SUBS + s) * n
                work[line : line + n, :] = new[:, 0:LANES]
                work[line + n : line + 2 * n, :] = new[:, LANES : 2 * LANES]
        solve_gains(z, flag, cross, lambda k: taper_ref[group[0], k], work, gains)
        for g in every:
            for k in range(n):
                work[pl.ds(g * SUBS * n + k, SUBS, stride=n), :] = gains[g * n + k]
            for s in range(0, SUBS, 2):
                line = (g * SUBS + s) * n
                k = [work[line : line + n, :], work[line + n : line + 2 * n, :]]
                k = jnp.concatenate(k, axis=1)
                high = k.astype(BF16)
                low = (k - high.astype(F32)).astype(BF16)
                total = dot(weight_ref[...], jnp.concatenate([high, low, high], axis=0))
                for t in range(2):
                    fl = (at * z.groups + g) * z.per_step + (s + t) // z.cells
                    off = shift_ref[pl.ds(fl, 1), :] * wet[s + t : s + t + 1, :]
                    rows = pl.ds(base + g * SUBS + s + t, z.members, stride=chunk)
                    flat_o[rows, :] = flat_x[rows, :] + (total[:, t * LANES : (t + 1) * LANES] - off)
        for copy in stores(at):
            copy.start()
        return carry

    lax.fori_loop(0, count, advance, 0)

    def drain(at, carry):
        for copy in stores(at):
            copy.wait()
        return carry

    lax.fori_loop(0, count, drain, 0)


def whole(*shape):
    return pl.BlockSpec(shape, lambda *_: (0,) * len(shape))


def smem():
    return pl.BlockSpec(memory_space=SMEM)


def struct(*shape, dtype=F32):
    return jax.ShapeDtypeStruct(shape, dtype)


def grant(mebibytes):
    return pltpu.CompilerParams(vmem_limit_bytes=mebibytes << 20)


def exchange(copies):
    return lax.all_to_all(copies, "domain", 0, 0, tiled=True)


def swap(z, array, x):
    return lax.ppermute(array, "member", [(p, p ^ x) for p in range(z.groups_m)])


def local(ensemble, velocity, diffusivity, land_mask, obs_index, obs_owner, obs_value, obs_error):
    z = Sizes(ensemble, obs_index)
    group = lax.axis_index("member").reshape(1)
    domain = lax.axis_index("domain").reshape(1)
    index = jnp.swapaxes(obs_index, 1, 2)
    state = ensemble.reshape(z.own, z.states, z.rows, z.cols)
    slab = pl.BlockSpec(memory_space=pltpu.HBM)
    held = [VMEM(state.shape, F32)]
    arrived = [pltpu.SemaphoreType.DMA((z.parts,))]
    side = pl.BlockSpec((z.rows, LANES), lambda i: (0, i))
    halo = z.parts * LANES
    first, last = pl.pallas_call(
        functools.partial(edges_kernel, z),
        grid=(z.parts,),
        in_specs=[slab],
        out_specs=[side] * 2,
        out_shape=[struct(z.rows, halo)] * 2,
        scratch_shapes=held + arrived,
        name="edges",
        compiler_params=grant(8),
    )(state)
    up = [(i, (i + 1) % z.groups_d) for i in range(z.groups_d)]
    down = [(j, i) for i, j in up]
    before = lax.ppermute(last, "domain", up)
    after = lax.ppermute(first, "domain", down)
    hbm = pl.BlockSpec(memory_space=pl.ANY)
    slots = range(1, z.groups_m)
    stepped, *moved, own_priors = pl.pallas_call(
        functools.partial(forecast_kernel, z),
        grid=(z.parts,),
        in_specs=[smem()] * 5
        + [
            slab,
            whole(z.rows, halo),
            whole(z.rows, halo),
            whole(*velocity.shape),
            whole(*land_mask.shape),
        ],
        out_specs=[hbm] * z.groups_m + [whole(SUBS, LANES)],
        out_shape=[struct(z.groups_m, z.own, z.lines, LANES)]
        + [struct(z.own, z.lines, LANES) for _ in slots]
        + [struct(SUBS, LANES)],
        scratch_shapes=held
        + [
            VMEM((z.groups_m, z.own, z.lines, LANES), F32),
            VMEM((z.window, LANES), F32),
            arrived[0],
            pltpu.SemaphoreType.DMA((z.groups_m, z.parts)),
        ],
        name="forecast",
        compiler_params=grant(16),
    )(group, domain, index, obs_owner, diffusivity, state, before, after, velocity, land_mask)
    priors = [own_priors] + [swap(z, own_priors, x) for x in slots]
    moved = [swap(z, slab, x) for x, slab in zip(slots, moved)]
    priors = jnp.broadcast_to(jnp.stack(priors)[None], (z.groups_d, z.groups_m, SUBS, LANES))
    priors = exchange(priors)
    n = z.obs
    vmem = pl.BlockSpec(memory_space=VMEM)
    gain, part, cross, flag, lift, tapers, relay, gap, wet = pl.pallas_call(
        functools.partial(filter_kernel, z),
        in_specs=[smem()] * 5 + [vmem, vmem],
        out_specs=[vmem] * 3 + [smem()] + [vmem] * 5,
        out_shape=[
            struct(n, 3 * z.members, dtype=BF16),
            struct(z.groups_m, n, 3 * z.window, dtype=BF16),
            struct(n, n),
            struct(z.batches, dtype=jnp.int32),
            struct(z.members, n),
            struct(z.groups_m, n, SUBS, LANES),
            struct(n, n),
            struct(SUBS, LANES),
            struct(z.groups_m, SUBS, LANES),
        ],
        name="filter",
        compiler_params=grant(8),
    )(domain, index, obs_owner, obs_value, obs_error, priors, land_mask)
    lines = z.groups * SUBS
    column = pl.BlockSpec((z.members, lines, LANES), lambda i: (0, i, 0))
    grid = (z.steps // z.groups,)
    work = VMEM((z.groups * SUBS * n, LANES), F32)
    gains = VMEM((z.groups * n, SUBS, LANES), F32)
    sums = pl.pallas_call(
        functools.partial(sums_kernel, z),
        grid=grid,
        in_specs=[
            smem(),
            smem(),
            smem(),
            column,
            whole(*part.shape),
            whole(*tapers.shape),
            whole(*wet.shape),
        ],
        out_specs=whole(z.groups_d, z.sum_rows + 1, LANES),
        out_shape=struct(z.groups_d, z.sum_rows + 1, LANES),
        scratch_shapes=[work, gains, gains, VMEM((z.sum_rows * LANES, LANES), F32)],
        name="sums",
        compiler_params=grant(12),
    )(group, cross, flag, stepped.reshape(z.members, z.lines, LANES), part, tapers, wet)
    sums = exchange(sums)
    sums = [sums] + [swap(z, sums, x) for x in slots]
    padded = z.states + -z.states % SUBS
    weight, shift = pl.pallas_call(
        functools.partial(weights_kernel, z),
        in_specs=[smem()] + [vmem] * (z.groups_m + 3),
        out_specs=[vmem] * 2,
        out_shape=[struct(z.members, 3 * n, dtype=BF16), struct(padded, LANES)],
        name="weights",
        compiler_params=grant(8),
    )(index, *sums, lift, relay, gap)
    sems = pltpu.SemaphoreType.DMA((z.groups_m, z.steps // z.groups))
    result = pl.pallas_call(
        functools.partial(update_kernel, z),
        in_specs=[smem()] * 3 + [hbm] * z.groups_m + [vmem] * 5,
        out_specs=hbm,
        out_shape=struct(z.members, z.lines, LANES),
        scratch_shapes=[VMEM((z.steps // z.groups, z.members, lines, LANES), F32)] * 2
        + [work, gains, sems, sems],
        name="update",
        compiler_params=grant(20),
    )(group, cross, flag, stepped, *moved, gain, tapers, wet, weight, shift)
    result = result.reshape(z.members, z.fields, z.levels, z.col_tiles, z.block_rows, LANES)
    result = jnp.swapaxes(result, 3, 4)
    return result.reshape(z.members, z.fields, z.levels, z.block_rows, z.cols)


def solution(mesh):
    in_specs = (
        P("member", None, None, None, "domain"),
        P(None, None, None, "domain"),
        P(),
        P(None, "domain"),
        P(),
        P(),
        P(),
        P(),
    )
    out_specs = P(None, None, None, "member", "domain")
    return jax.shard_map(local, mesh=mesh, in_specs=in_specs, out_specs=out_specs, check_vma=False)
```

```python
import functools

import jax
import jax.numpy as jnp
from jax import lax
from jax.experimental import pallas as pl
from jax.experimental.pallas import tpu as pltpu
from jax.sharding import PartitionSpec as P


LOC_RADIUS = 64
LANES = 128
SUBS = 8
F32 = jnp.float32
BF16 = jnp.bfloat16
HIGHEST = lax.Precision.HIGHEST
VMEM = pltpu.VMEM
SMEM = pltpu.SMEM


def gaspari(scaled):
    scaled_safe = jnp.maximum(scaled, 1.0)
    near_part = (
        ((-0.25 * scaled + 0.5) * scaled + 0.625) * scaled - 5.0 / 3.0
    ) * scaled * scaled + 1.0
    far_part = (
        ((((scaled / 12.0 - 0.5) * scaled + 0.625) * scaled + 5.0 / 3.0) * scaled - 5.0) * scaled
        + 4.0
        - 2.0 / (3.0 * scaled_safe)
    )
    return jnp.where(scaled <= 1.0, near_part, jnp.where(scaled < 2.0, far_part, 0.0))


def taper(row_gap, col_gap, grid_width):
    col_gap = jnp.abs(col_gap)
    col_gap = jnp.minimum(col_gap, grid_width - col_gap)
    square = (col_gap * col_gap + row_gap * row_gap).astype(F32)
    return gaspari(jnp.sqrt(square) * (1.0 / LOC_RADIUS))


def iota(shape, dim):
    return lax.broadcasted_iota(jnp.int32, shape, dim)


def split(value):
    high = value.astype(BF16)
    return high, (value - high.astype(F32)).astype(BF16)


def dot(a, b):
    return lax.dot_general(a, b, (((1,), (0,)), ((), ())), preferred_element_type=F32)


def dot_exact(a, b, dims):
    return lax.dot_general(
        a, b, ((dims[:1], dims[1:]), ((), ())), precision=HIGHEST, preferred_element_type=F32
    )


class Sizes:
    def __init__(self, ensemble, obs_index):
        self.own, self.fields, self.levels, self.rows, self.cols = ensemble.shape
        self.states = self.fields * self.levels
        self.groups_m = lax.axis_size("member")
        self.groups_d = lax.axis_size("domain")
        self.members = self.own * self.groups_m
        self.block_rows = self.rows // self.groups_m
        self.col_tiles = self.cols // LANES
        self.cells = self.block_rows * self.col_tiles
        self.per_step = SUBS // self.cells
        self.steps = self.states // self.per_step
        self.width = self.cols * self.groups_d
        self.batches, self.batch = obs_index.shape[:2]
        self.obs = self.batches * self.batch
        self.pack_states = LANES // self.obs
        self.sum_rows = -(-self.states // self.pack_states)
        self.part = next(m for m in (5, 4, 3, 2, 1) if self.own % m == 0)
        self.parts = self.own // self.part
        self.lines = self.states * self.cells
        self.groups = next(g for g in (3, 2, 1) if self.steps % g == 0)
        self.window = -(-self.own // SUBS) * SUBS

    def start(self, p):
        return min(p * self.own, self.members - self.window)


def arrivals(z, step, given, source, sems):
    def copy(at):
        part = pl.ds(at * z.part, z.part)
        return pltpu.make_async_copy(given.at[part], source.at[part], sems.at[at])

    @pl.when(step == 0)
    def _():
        for at in range(z.parts):
            copy(at).start()

    copy(step).wait()


def edges_kernel(z, given, first_ref, last_ref, source, sems):
    step = pl.program_id(0)
    arrivals(z, step, given, source, sems)
    lane = iota((z.rows, LANES), 1)
    first = jnp.zeros((z.rows, LANES), F32)
    last = first
    for m in range(z.part):
        for fl in range(z.states):
            hit = lane == m * z.states + fl
            at = step * z.part + m
            first = jnp.where(hit, source[at, fl, :, 0:1], first)
            last = jnp.where(hit, source[at, fl, :, z.cols - 1 : z.cols], last)
    first_ref[...] = first
    last_ref[...] = last


def forecast_kernel(
    z, group, domain, index, owner, diff, given, before_ref, after_ref, vel_ref, mask_ref,
    state, *refs,
):
    others = refs[: z.groups_m - 1]
    obs_ref, picked, source, in_sems = refs[z.groups_m - 1 :]
    step = pl.program_id(0)
    arrivals(z, step, given, source, in_sems)
    shape = (z.rows, z.cols)
    row, col = iota(shape, 0), iota(shape, 1)
    wet = mask_ref[...].astype(F32)
    flat = state.reshape(z.members * z.lines, LANES)
    member = pl.multiple_of(step * (z.part * z.lines), SUBS)
    side = pl.ds(pl.multiple_of(step * LANES, LANES), LANES)
    before = before_ref[:, side]
    after = after_ref[:, side]
    for fl in range(z.states):
        level = fl % z.levels
        spread = diff[fl // z.levels]
        half_u = 0.5 * vel_ref[0, level]
        half_v = 0.5 * vel_ref[1, level]
        center = wet * (1.0 - 4.0 * spread)
        east = wet * (spread - half_u)
        west = wet * (spread + half_u)
        north = jnp.where(row == z.rows - 1, 0.0, wet * (spread - half_v))
        south = jnp.where(row == 0, 0.0, wet * (spread + half_v))
        for m in range(z.part):
            x = source[step * z.part + m, fl]
            at = m * z.states + fl
            nxt = jnp.where(col == z.cols - 1, after[:, at : at + 1], pltpu.roll(x, z.cols - 1, 1))
            prv = jnp.where(col == 0, before[:, at : at + 1], pltpu.roll(x, 1, 1))
            y = (
                center * x
                + east * nxt
                + west * prv
                + north * pltpu.roll(x, z.rows - 1, 0)
                + south * pltpu.roll(x, 1, 0)
            )
            for p in range(z.groups_m):
                for c in range(z.col_tiles):
                    line = (p * z.own + m) * z.lines + fl * z.cells + c * z.block_rows
                    flat[pl.ds(member + line, z.block_rows), :] = y[
                        p * z.block_rows : (p + 1) * z.block_rows, c * LANES : (c + 1) * LANES
                    ]

    part = pl.ds(step * z.part, z.part)
    for x, other in enumerate(others, 1):
        other[part] = state[jnp.bitwise_xor(group[0], x), part]

    @pl.when(step == z.parts - 1)
    def _():
        picked[...] = jnp.zeros_like(picked)
        lane = iota((z.own, LANES), 1)
        for b in range(z.batches):

            @pl.when(lax.rem(owner[b], z.groups_d) == domain[0])
            def _():
                total = picked[0 : z.own, :]
                first = owner[b] // z.groups_d * z.own * z.lines
                for i in range(z.batch):
                    fl = index[b, 0, i] * z.levels + index[b, 1, i]
                    at = index[b, 3, i]
                    cell = (at // LANES) * z.block_rows + index[b, 2, i]
                    got = flat[pl.ds(first + fl * z.cells + cell, z.own, stride=z.lines), :]
                    at = lax.rem(at, LANES)
                    got = jnp.where(lane == at, got, 0.0)
                    turn = lax.rem(b * z.batch + i + LANES - at, LANES)
                    total = total + pltpu.roll(got, turn, 1)
                picked[0 : z.own, :] = total

        total = picked[0:SUBS, :]
        for v in range(1, z.window // SUBS):
            total = total + pltpu.roll(picked[v * SUBS : (v + 1) * SUBS, :], v * z.obs, 1)
        obs_ref[...] = total


def tapers_kernel(z, domain, index, owner, mask_ref, taper_ref, wet_ref, mutual_ref, flag):
    n = z.obs
    square = (n, LANES)
    row, lane = iota(square, 0), iota(square, 1)
    rows_s, cols_s = jnp.zeros(square, jnp.int32), jnp.zeros(square, jnp.int32)
    rows_l, cols_l = rows_s, cols_s
    shape = (SUBS, LANES)
    sub = iota(shape, 0) % z.cells
    cell_row = sub % z.block_rows
    first_col = domain[0] * z.cols
    cell_col = first_col + (sub // z.block_rows) * LANES + iota(shape, 1)
    wets = []
    for p in range(z.groups_m):
        wet = jnp.zeros(shape, F32)
        for c in range(z.col_tiles):
            for r in range(z.block_rows):
                full_row = p * z.block_rows + r
                line = mask_ref[full_row : full_row + 1, c * LANES : (c + 1) * LANES]
                wet = jnp.where(sub == c * z.block_rows + r, line.astype(F32), wet)
        wet_ref[p] = wet
        wets.append(wet)
    for b in range(z.batches):
        near = jnp.int32(0)
        tile = lax.rem(owner[b], z.groups_d) * z.cols
        first_row = owner[b] // z.groups_d * z.block_rows
        for i in range(z.batch):
            k = b * z.batch + i
            at_row = first_row + index[b, 2, i]
            at_col = tile + index[b, 3, i]
            rows_s = jnp.where(row == k, at_row, rows_s)
            cols_s = jnp.where(row == k, at_col, cols_s)
            rows_l = jnp.where(lane == k, at_row, rows_l)
            cols_l = jnp.where(lane == k, at_col, cols_l)
            ahead = lax.rem(at_col - first_col + z.width, z.width)
            behind = z.width - ahead
            reach = 2 * LOC_RADIUS
            close = (ahead < z.cols + reach) | (behind < reach)
            near = jnp.where(close, 1, near)
        flag[b] = near

        @pl.when(near > 0)
        def _():
            for i in range(z.batch):
                k = b * z.batch + i
                at_row = first_row + index[b, 2, i]
                at_col = tile + index[b, 3, i]
                for p in range(z.groups_m):
                    rho = taper(cell_row + (p * z.block_rows - at_row), cell_col - at_col, z.width)
                    taper_ref[p, k] = wets[p] * rho
    mutual_ref[...] = taper(rows_s - rows_l, cols_s - cols_l, z.width)


def filter_kernel(
    z, value, error, got_ref, mutual_ref,
    gain_ref, part_ref, cross_ref, lift_ref, relay_ref, gap_ref,
):
    n = z.obs
    eight = z.groups_m * SUBS
    stacked = []
    for x in range(z.groups_m):
        total = got_ref[0, x]
        for d in range(1, z.groups_d):
            total = total + got_ref[d, x]
        stacked.append(total)
    stacked = jnp.concatenate(stacked, axis=0)
    square = (n, LANES)
    prior = jnp.zeros(square, F32)
    row, lane = iota(square, 0), iota(square, 1)
    for v in range(z.window // SUBS):
        pick = (lane == row + v * n).astype(F32)
        part = dot_exact(pick, stacked, (1, 1))
        src = iota((eight, LANES), 0)
        dst = iota((eight, LANES), 1)
        slot = v * SUBS + src % SUBS
        place_of = jnp.where(slot < z.own, (src // SUBS) * z.own + slot, -1)
        prior = prior + dot_exact(part, (dst == place_of).astype(F32), (1, 0))
    ones = jnp.full((SUBS, LANES), 1.0 / z.members, F32)
    mean_row = dot_exact(ones, prior, (1, 1))
    mean = jnp.sum(prior, axis=1, keepdims=True) * (1.0 / z.members)
    anomaly = jnp.where(lane < z.members, prior - mean, 0.0)
    values = jnp.zeros((SUBS, n), F32)
    value_lane = iota((SUBS, n), 1)
    for k in range(n):
        values = jnp.where(value_lane == k, value[k // z.batch, k % z.batch], values)
    gap_ref[...] = jnp.zeros_like(gap_ref)
    gap_ref[:, 0:n] = values - mean_row
    mutual = mutual_ref[...]
    relay = jnp.zeros(square, F32)
    inverse_l = jnp.zeros(square, F32)
    inverse_s = jnp.zeros(square, F32)
    shrink_s = jnp.zeros(square, F32)
    spread = float(z.members - 1)
    for k in range(n):
        b, i = divmod(k, z.batch)
        own = anomaly[k : k + 1, :]
        product = jnp.sum(anomaly * own, axis=1, keepdims=True)
        variance = product[k : k + 1, :] * (1.0 / spread) + error[b, i]
        inverse = 1.0 / (spread * variance)
        shrink = 1.0 / (1.0 + jnp.sqrt(error[b, i] / variance))
        ratio = jnp.where(row[:, 0:1] > k, mutual[:, k : k + 1] * product * inverse, 0.0)
        anomaly = anomaly - (shrink * ratio) * own
        relay = jnp.where(lane == k, ratio, relay)
        inverse_l = jnp.where(lane == k, inverse, inverse_l)
        inverse_s = jnp.where(row == k, inverse, inverse_s)
        shrink_s = jnp.where(row == k, shrink, shrink_s)
    gram = dot_exact(anomaly, anomaly, (1, 1))
    cross_ref[...] = -shrink_s[:, 0:n] * inverse_l[:, 0:n] * gram
    high, low = split(anomaly * inverse_s)

    def tripled(count, offset, width):
        shape = (LANES, 3 * width)
        src, dst = iota(shape, 0), iota(shape, 1)
        third, slot = dst // width, dst % width - offset
        hit = (src == slot) & (slot >= 0) & (slot < count)
        upper = (hit & (third < 2)).astype(BF16)
        lower = (hit & (third == 2)).astype(BF16)
        return (dot(high, upper) + dot(low, lower)).astype(BF16)

    gain_ref[...] = tripled(z.members, 0, z.members)
    made = {}
    for p in range(z.groups_m):
        offset = p * z.own - z.start(p)
        if offset not in made:
            made[offset] = tripled(z.own, offset, z.window)
        part_ref[p] = made[offset]
    eye = (iota((z.members, LANES), 0) == iota((z.members, LANES), 1)).astype(F32)
    lift_ref[...] = dot_exact(eye, shrink_s * anomaly, (1, 1))
    eye = (iota((n, LANES), 0) == iota((n, LANES), 1)).astype(F32)
    relay_ref[...] = dot_exact(eye, relay, (1, 1))


def stacked_rows(flat, first, count, lines):
    x = [flat[pl.ds(first + t, count, stride=lines), :] for t in range(2)]
    x = jnp.concatenate(x, axis=1)
    high = x.astype(BF16).astype(F32)
    return jnp.concatenate([high, x - high, high], axis=0).astype(BF16)


def solve_gains(z, flag, cross, taper_of, work, gains):
    n, size = z.obs, z.batch
    every = range(z.groups)

    for b in range(z.batches):

        @pl.when(flag[b] > 0)
        def _():
            part = [
                [work[pl.ds(g * SUBS * n + b * size + i, SUBS, stride=n), :] for g in every]
                for i in range(size)
            ]
            for before in range(b):

                def add(part):
                    part = [list(each) for each in part]
                    for j in range(before * size, (before + 1) * size):
                        held = [gains[g * n + j] for g in every]
                        for i in range(size):
                            factor = cross[j, b * size + i]
                            for g in every:
                                part[i][g] = part[i][g] + factor * held[g]
                    return part

                part = lax.cond(flag[before] > 0, add, lambda part: part, part)
            for i in range(size):
                k = b * size + i
                rho = taper_of(k)
                for g in every:
                    kalman = rho * part[i][g]
                    gains[g * n + k] = kalman
                    for j in range(i + 1, size):
                        part[j][g] = part[j][g] + cross[k, b * size + j] * kalman

        @pl.when(flag[b] == 0)
        def _():
            for i in range(size):
                for g in every:
                    gains[g * n + b * size + i] = jnp.zeros((SUBS, LANES), F32)


def sums_kernel(
    z, group, cross, flag, x_ref, part_ref, taper_ref, wet_ref, sums_ref, work, gains, total, held
):
    n = z.obs
    step = pl.program_id(0)
    lines = z.lines
    flat = x_ref.reshape(z.members * lines, LANES)
    first_line = pl.multiple_of(step * (z.groups * SUBS), SUBS)
    total[...] = jnp.zeros_like(total)
    every = range(z.groups)

    for p in range(z.groups_m):
        for g in every:
            for s in range(0, SUBS, 2):
                first = first_line + z.start(p) * lines + g * SUBS + s
                x = stacked_rows(flat, first, z.window, lines)
                got = dot(part_ref[p], x)
                at = (g * SUBS + s) * n
                work[at : at + n, :] = got[:, 0:LANES]
                work[at + n : at + 2 * n, :] = got[:, LANES : 2 * LANES]
        solve_gains(z, flag, cross, lambda k: taper_ref[p, k], work, gains)
        for g in every:
            for k in range(n):
                total[g * n + k] = total[g * n + k] + gains[g * n + k]
    for g in every:
        for k in range(n):
            work[pl.ds(g * SUBS * n + k, SUBS, stride=n), :] = total[g * n + k]
        for q in range(z.per_step):
            first = g * SUBS + q * z.cells
            each = work[first * n : (first + 1) * n, :]
            for s in range(first + 1, first + z.cells):
                each = each + work[s * n : (s + 1) * n, :]
            fl = (step * z.groups + g) * z.per_step + q
            held[pl.ds(pl.multiple_of(fl * n, n), n), :] = each

    @pl.when(step == z.steps // z.groups - 1)
    def _():
        ones = jnp.ones((SUBS, LANES), F32)
        wet = jnp.sum(wet_ref[group[0]][0 : z.cells, :], axis=0, keepdims=True)
        rows = [
            dot_exact(ones, held[i * LANES : (i + 1) * LANES, :], (1, 1))[0:1, :]
            for i in range(z.sum_rows)
        ]
        rows.append(wet)
        for d in range(z.groups_d):
            for i, line in enumerate(rows):
                sums_ref[d, i : i + 1, :] = line


def weights_kernel(z, index, *refs):
    lift_ref, relay_ref, gap_ref, weight_ref, shift_ref = refs[z.groups_m :]
    n = z.obs
    sums = sum(ref[d] for ref in refs[: z.groups_m] for d in range(z.groups_d))
    count = jnp.sum(sums[z.sum_rows : z.sum_rows + 1, :], axis=1, keepdims=True)
    lines = []
    for fl in range(z.states):
        i, c = divmod(fl, z.pack_states)
        lines.append(sums[i : i + 1, c * n : (c + 1) * n])
    pad = -z.states % SUBS
    table = jnp.concatenate(lines + [jnp.zeros((pad, n), F32)], axis=0) / count
    eye = (iota((n, n), 0) == iota((n, n), 1)).astype(F32)
    turned = dot_exact(eye, table, (1, 1))
    shape = (z.states + pad, n)
    fl_row, lane = iota(shape, 0), iota(shape, 1)
    at = jnp.zeros(shape, jnp.int32)
    for k in range(n):
        b, i = divmod(k, z.batch)
        at = jnp.where(lane == k, index[b, 0, i] * z.levels + index[b, 1, i], at)
    chosen = dot_exact(turned, (fl_row == at).astype(F32), (1, 0))
    later = iota((n, n), 1) // z.batch > iota((n, n), 0) // z.batch
    relay = relay_ref[...] - jnp.where(later, chosen, 0.0)
    gap = gap_ref[0:1, 0:n]
    for k in range(n):
        gap = gap - gap[:, k : k + 1] * relay[k : k + 1, :]
    shift = jnp.sum(table * gap, axis=1, keepdims=True)
    shift_ref[...] = jnp.broadcast_to(shift, shift_ref.shape)
    high, low = split(gap - lift_ref[...])
    src, dst = iota((n, 3 * n), 0), iota((n, 3 * n), 1)
    hit = src == dst % n
    upper = (hit & (dst < 2 * n)).astype(BF16)
    lower = (hit & (dst >= 2 * n)).astype(BF16)
    weight_ref[...] = (dot(high, upper) + dot(low, lower)).astype(BF16)


def update_kernel(z, group, cross, flag, *refs):
    n = z.obs
    slabs = refs[: z.groups_m]
    gain_ref, taper_ref, wet_ref, weight_ref, shift_ref, out_ref = refs[z.groups_m : -5]
    got, made, work, gains, out_sems = refs[-5:]
    chunk = z.groups * SUBS
    flat_x = got.reshape(z.members * chunk, LANES)
    flat_o = made.reshape(z.members * z.lines, LANES)
    size = z.members * chunk
    every = range(z.groups)

    def lines(at):
        return pl.ds(pl.multiple_of(at * chunk, SUBS), chunk)

    def stores(at):
        for x in range(z.groups_m):
            first = jnp.bitwise_xor(group[0], x) * z.own
            here = made.at[at, x * z.own : (x + 1) * z.own]
            there = out_ref.at[pl.ds(first, z.own), lines(at)]
            yield pltpu.make_async_copy(here, there, out_sems.at[x, at])

    count = z.steps // z.groups
    wet = wet_ref[group[0]]

    def advance(at, carry):
        for x, slab in enumerate(slabs):
            src = slab.at[group[0]] if x == 0 else slab
            got[x * z.own : (x + 1) * z.own] = src[:, lines(at)]
        base = pl.multiple_of(at * size, SUBS)
        for g in every:
            for s in range(0, SUBS, 2):
                x = stacked_rows(flat_x, g * SUBS + s, z.members, chunk)
                new = dot(gain_ref[...], x)
                line = (g * SUBS + s) * n
                work[line : line + n, :] = new[:, 0:LANES]
                work[line + n : line + 2 * n, :] = new[:, LANES : 2 * LANES]
        solve_gains(z, flag, cross, lambda k: taper_ref[group[0], k], work, gains)
        for g in every:
            for k in range(n):
                work[pl.ds(g * SUBS * n + k, SUBS, stride=n), :] = gains[g * n + k]
            for s in range(0, SUBS, 2):
                line = (g * SUBS + s) * n
                k = [work[line : line + n, :], work[line + n : line + 2 * n, :]]
                k = jnp.concatenate(k, axis=1)
                high = k.astype(BF16)
                low = (k - high.astype(F32)).astype(BF16)
                total = dot(weight_ref[...], jnp.concatenate([high, low, high], axis=0))
                for t in range(2):
                    fl = (at * z.groups + g) * z.per_step + (s + t) // z.cells
                    off = shift_ref[pl.ds(fl, 1), :] * wet[s + t : s + t + 1, :]
                    line = g * SUBS + s + t
                    old = flat_x[pl.ds(line, z.members, stride=chunk), :]
                    new = old + (total[:, t * LANES : (t + 1) * LANES] - off)
                    flat_o[pl.ds(base + line, z.members, stride=chunk), :] = new
        for copy in stores(at):
            copy.start()
        return carry

    lax.fori_loop(0, count, advance, 0)

    def drain(at, carry):
        for copy in stores(at):
            copy.wait()
        return carry

    lax.fori_loop(0, count, drain, 0)


def whole(*shape):
    return pl.BlockSpec(shape, lambda *_: (0,) * len(shape))


def smem():
    return pl.BlockSpec(memory_space=SMEM)


def struct(*shape, dtype=F32):
    return jax.ShapeDtypeStruct(shape, dtype)


def grant(mebibytes):
    return pltpu.CompilerParams(vmem_limit_bytes=mebibytes << 20)


def exchange(copies):
    return lax.all_to_all(copies, "domain", 0, 0, tiled=True)


def swap(z, array, x):
    return lax.ppermute(array, "member", [(p, p ^ x) for p in range(z.groups_m)])


def local(ensemble, velocity, diffusivity, land_mask, obs_index, obs_owner, obs_value, obs_error):
    z = Sizes(ensemble, obs_index)
    group = lax.axis_index("member").reshape(1)
    domain = lax.axis_index("domain").reshape(1)
    index = jnp.swapaxes(obs_index, 1, 2)
    state = ensemble.reshape(z.own, z.states, z.rows, z.cols)
    vmem = pl.BlockSpec(memory_space=VMEM)
    state = pltpu.with_memory_space_constraint(state, pltpu.HBM)
    side = pl.BlockSpec((z.rows, LANES), lambda i: (0, i))
    halo = z.parts * LANES
    hbm = pl.BlockSpec(memory_space=pl.ANY)
    arrived = [VMEM(state.shape, F32), pltpu.SemaphoreType.DMA((z.parts,))]
    first, last = pl.pallas_call(
        functools.partial(edges_kernel, z),
        grid=(z.parts,),
        in_specs=[hbm],
        out_specs=[side] * 2,
        out_shape=[struct(z.rows, halo)] * 2,
        scratch_shapes=arrived,
        name="edges",
        compiler_params=grant(12),
    )(state)
    up = [(i, (i + 1) % z.groups_d) for i in range(z.groups_d)]
    down = [(j, i) for i, j in up]
    before = lax.ppermute(last, "domain", up)
    after = lax.ppermute(first, "domain", down)
    n = z.obs
    tapers, wet, mutual, flag = pl.pallas_call(
        functools.partial(tapers_kernel, z),
        in_specs=[smem()] * 3 + [vmem],
        out_specs=[vmem] * 3 + [smem()],
        out_shape=[
            struct(z.groups_m, n, SUBS, LANES),
            struct(z.groups_m, SUBS, LANES),
            struct(n, LANES),
            struct(z.batches, dtype=jnp.int32),
        ],
        name="tapers",
        compiler_params=grant(8),
    )(domain, index, obs_owner, land_mask)
    slots = range(1, z.groups_m)
    stepped, *moved, own_priors = pl.pallas_call(
        functools.partial(forecast_kernel, z),
        grid=(z.parts,),
        in_specs=[smem()] * 5
        + [
            hbm,
            whole(z.rows, halo),
            whole(z.rows, halo),
            whole(*velocity.shape),
            whole(*land_mask.shape),
        ],
        out_specs=[vmem] * z.groups_m + [whole(SUBS, LANES)],
        out_shape=[struct(z.groups_m, z.own, z.lines, LANES)]
        + [struct(z.own, z.lines, LANES) for _ in slots]
        + [struct(SUBS, LANES)],
        scratch_shapes=[
            VMEM((z.window, LANES), F32),
        ]
        + arrived,
        name="forecast",
        compiler_params=grant(20),
    )(group, domain, index, obs_owner, diffusivity, state, before, after, velocity, land_mask)
    priors = [own_priors] + [swap(z, own_priors, x) for x in slots]
    moved = [swap(z, slab, x) for x, slab in zip(slots, moved)]
    priors = jnp.broadcast_to(jnp.stack(priors)[None], (z.groups_d, z.groups_m, SUBS, LANES))
    priors = exchange(priors)
    gain, part, cross, lift, relay, gap = pl.pallas_call(
        functools.partial(filter_kernel, z),
        in_specs=[smem()] * 2 + [vmem] * 2,
        out_specs=[vmem] * 6,
        out_shape=[
            struct(n, 3 * z.members, dtype=BF16),
            struct(z.groups_m, n, 3 * z.window, dtype=BF16),
            struct(n, n),
            struct(z.members, n),
            struct(n, n),
            struct(SUBS, LANES),
        ],
        name="filter",
        compiler_params=grant(8),
    )(obs_value, obs_error, priors, mutual)
    lines = z.groups * SUBS
    grid = (z.steps // z.groups,)
    work = VMEM((z.groups * SUBS * n, LANES), F32)
    gains = VMEM((z.groups * n, SUBS, LANES), F32)
    sums = pl.pallas_call(
        functools.partial(sums_kernel, z),
        grid=grid,
        in_specs=[
            smem(),
            smem(),
            smem(),
            vmem,
            vmem,
            vmem,
            vmem,
        ],
        out_specs=whole(z.groups_d, z.sum_rows + 1, LANES),
        out_shape=struct(z.groups_d, z.sum_rows + 1, LANES),
        scratch_shapes=[work, gains, gains, VMEM((z.sum_rows * LANES, LANES), F32)],
        name="sums",
        compiler_params=grant(12),
    )(group, cross, flag, stepped.reshape(z.members, z.lines, LANES), part, tapers, wet)
    sums = exchange(sums)
    sums = [sums] + [swap(z, sums, x) for x in slots]
    padded = z.states + -z.states % SUBS
    weight, shift = pl.pallas_call(
        functools.partial(weights_kernel, z),
        in_specs=[smem()] + [vmem] * (z.groups_m + 3),
        out_specs=[vmem] * 2,
        out_shape=[struct(z.members, 3 * n, dtype=BF16), struct(padded, LANES)],
        name="weights",
        compiler_params=grant(8),
    )(index, *sums, lift, relay, gap)
    sems = pltpu.SemaphoreType.DMA((z.groups_m, z.steps // z.groups))
    result = pl.pallas_call(
        functools.partial(update_kernel, z),
        in_specs=[smem()] * 3 + [vmem] * (z.groups_m + 5),
        out_specs=hbm,
        out_shape=struct(z.members, z.lines, LANES),
        scratch_shapes=[
            VMEM((z.members, lines, LANES), F32),
            VMEM((z.steps // z.groups, z.members, lines, LANES), F32),
            work,
            gains,
            sems,
        ],
        name="update",
        compiler_params=grant(20),
    )(group, cross, flag, stepped, *moved, gain, tapers, wet, weight, shift)
    result = result.reshape(z.members, z.fields, z.levels, z.col_tiles, z.block_rows, LANES)
    result = jnp.swapaxes(result, 3, 4)
    return result.reshape(z.members, z.fields, z.levels, z.block_rows, z.cols)


def solution(mesh):
    in_specs = (
        P("member", None, None, None, "domain"),
        P(None, None, None, "domain"),
        P(),
        P(None, "domain"),
        P(),
        P(),
        P(),
        P(),
    )
    out_specs = P(None, None, None, "member", "domain")
    return jax.shard_map(local, mesh=mesh, in_specs=in_specs, out_specs=out_specs, check_vma=False)
```

```python
import functools

import jax
import jax.numpy as jnp
from jax import lax
from jax.experimental import pallas as pl
from jax.experimental.pallas import tpu as pltpu
from jax.sharding import PartitionSpec as P


LOC_RADIUS = 64
LANES = 128
SUBS = 8
F32 = jnp.float32
BF16 = jnp.bfloat16
HIGHEST = lax.Precision.HIGHEST
VMEM = pltpu.VMEM
SMEM = pltpu.SMEM


def gaspari(scaled):
    scaled_safe = jnp.maximum(scaled, 1.0)
    near_part = (
        ((-0.25 * scaled + 0.5) * scaled + 0.625) * scaled - 5.0 / 3.0
    ) * scaled * scaled + 1.0
    far_part = (
        ((((scaled / 12.0 - 0.5) * scaled + 0.625) * scaled + 5.0 / 3.0) * scaled - 5.0) * scaled
        + 4.0
        - 2.0 / (3.0 * scaled_safe)
    )
    return jnp.where(scaled <= 1.0, near_part, jnp.where(scaled < 2.0, far_part, 0.0))


def taper(row_gap, col_gap, grid_width):
    col_gap = jnp.abs(col_gap)
    col_gap = jnp.minimum(col_gap, grid_width - col_gap)
    square = (col_gap * col_gap + row_gap * row_gap).astype(F32)
    return gaspari(jnp.sqrt(square) * (1.0 / LOC_RADIUS))


def iota(shape, dim):
    return lax.broadcasted_iota(jnp.int32, shape, dim)


def split(value):
    high = value.astype(BF16)
    return high, (value - high.astype(F32)).astype(BF16)


def dot(a, b):
    return lax.dot_general(a, b, (((1,), (0,)), ((), ())), preferred_element_type=F32)


def dot_exact(a, b, dims):
    return lax.dot_general(
        a, b, ((dims[:1], dims[1:]), ((), ())), precision=HIGHEST, preferred_element_type=F32
    )


class Sizes:
    def __init__(self, ensemble, obs_index):
        self.own, self.fields, self.levels, self.rows, self.cols = ensemble.shape
        self.states = self.fields * self.levels
        self.groups_m = lax.axis_size("member")
        self.groups_d = lax.axis_size("domain")
        self.members = self.own * self.groups_m
        self.block_rows = self.rows // self.groups_m
        self.col_tiles = self.cols // LANES
        self.cells = self.block_rows * self.col_tiles
        self.per_step = SUBS // self.cells
        self.steps = self.states // self.per_step
        self.width = self.cols * self.groups_d
        self.batches, self.batch = obs_index.shape[:2]
        self.obs = self.batches * self.batch
        self.pack_states = LANES // self.obs
        self.sum_rows = -(-self.states // self.pack_states)
        self.part = next(m for m in (5, 4, 3, 2, 1) if self.own % m == 0)
        self.parts = self.own // self.part
        self.lines = self.states * self.cells
        self.groups = next(g for g in (3, 2, 1) if self.steps % g == 0)
        self.window = -(-self.own // SUBS) * SUBS

    def start(self, p):
        return min(p * self.own, self.members - self.window)


def arrivals(z, step, given, source, sems):
    def copy(at):
        part = pl.ds(at * z.part, z.part)
        return pltpu.make_async_copy(given.at[part], source.at[part], sems.at[at])

    @pl.when(step == 0)
    def _():
        for at in range(z.parts):
            copy(at).start()

    copy(step).wait()


def edges_kernel(z, given, first_ref, last_ref, source, sems):
    step = pl.program_id(0)
    arrivals(z, step, given, source, sems)
    lane = iota((z.rows, LANES), 1)
    first = jnp.zeros((z.rows, LANES), F32)
    last = first
    for m in range(z.part):
        for fl in range(z.states):
            hit = lane == m * z.states + fl
            at = step * z.part + m
            first = jnp.where(hit, source[at, fl, :, 0:1], first)
            last = jnp.where(hit, source[at, fl, :, z.cols - 1 : z.cols], last)
    first_ref[...] = first
    last_ref[...] = last


def forecast_kernel(
    z, group, domain, index, owner, diff, given, before_ref, after_ref, vel_ref, mask_ref,
    state, *refs,
):
    others = refs[: z.groups_m - 1]
    obs_ref, picked, source, in_sems = refs[z.groups_m - 1 :]
    step = pl.program_id(0)
    arrivals(z, step, given, source, in_sems)
    shape = (z.rows, z.cols)
    row, col = iota(shape, 0), iota(shape, 1)
    wet = mask_ref[...].astype(F32)
    flat = state.reshape(z.members * z.lines, LANES)
    member = pl.multiple_of(step * (z.part * z.lines), SUBS)
    side = pl.ds(pl.multiple_of(step * LANES, LANES), LANES)
    before = before_ref[:, side]
    after = after_ref[:, side]
    for fl in range(z.states):
        level = fl % z.levels
        spread = diff[fl // z.levels]
        half_u = 0.5 * vel_ref[0, level]
        half_v = 0.5 * vel_ref[1, level]
        center = wet * (1.0 - 4.0 * spread)
        east = wet * (spread - half_u)
        west = wet * (spread + half_u)
        north = jnp.where(row == z.rows - 1, 0.0, wet * (spread - half_v))
        south = jnp.where(row == 0, 0.0, wet * (spread + half_v))
        for m in range(z.part):
            x = source[step * z.part + m, fl]
            at = m * z.states + fl
            nxt = jnp.where(col == z.cols - 1, after[:, at : at + 1], pltpu.roll(x, z.cols - 1, 1))
            prv = jnp.where(col == 0, before[:, at : at + 1], pltpu.roll(x, 1, 1))
            y = (
                center * x
                + east * nxt
                + west * prv
                + north * pltpu.roll(x, z.rows - 1, 0)
                + south * pltpu.roll(x, 1, 0)
            )
            for p in range(z.groups_m):
                for c in range(z.col_tiles):
                    line = (p * z.own + m) * z.lines + fl * z.cells + c * z.block_rows
                    flat[pl.ds(member + line, z.block_rows), :] = y[
                        p * z.block_rows : (p + 1) * z.block_rows, c * LANES : (c + 1) * LANES
                    ]

    part = pl.ds(step * z.part, z.part)
    for x, other in enumerate(others, 1):
        other[part] = state[jnp.bitwise_xor(group[0], x), part]

    @pl.when(step == z.parts - 1)
    def _():
        picked[...] = jnp.zeros_like(picked)
        lane = iota((z.own, LANES), 1)
        for b in range(z.batches):

            @pl.when(lax.rem(owner[b], z.groups_d) == domain[0])
            def _():
                total = picked[0 : z.own, :]
                first = owner[b] // z.groups_d * z.own * z.lines
                for i in range(z.batch):
                    fl = index[b, 0, i] * z.levels + index[b, 1, i]
                    at = index[b, 3, i]
                    cell = (at // LANES) * z.block_rows + index[b, 2, i]
                    got = flat[pl.ds(first + fl * z.cells + cell, z.own, stride=z.lines), :]
                    at = lax.rem(at, LANES)
                    got = jnp.where(lane == at, got, 0.0)
                    turn = lax.rem(b * z.batch + i + LANES - at, LANES)
                    total = total + pltpu.roll(got, turn, 1)
                picked[0 : z.own, :] = total

        total = picked[0:SUBS, :]
        for v in range(1, z.window // SUBS):
            total = total + pltpu.roll(picked[v * SUBS : (v + 1) * SUBS, :], v * z.obs, 1)
        obs_ref[...] = total


def tapers_kernel(z, domain, index, owner, mask_ref, taper_ref, wet_ref, mutual_ref, flag):
    n = z.obs
    square = (n, LANES)
    row, lane = iota(square, 0), iota(square, 1)
    rows_s, cols_s = jnp.zeros(square, jnp.int32), jnp.zeros(square, jnp.int32)
    rows_l, cols_l = rows_s, cols_s
    shape = (SUBS, LANES)
    sub = iota(shape, 0) % z.cells
    cell_row = sub % z.block_rows
    first_col = domain[0] * z.cols
    cell_col = first_col + (sub // z.block_rows) * LANES + iota(shape, 1)
    wets = []
    for p in range(z.groups_m):
        wet = jnp.zeros(shape, F32)
        for c in range(z.col_tiles):
            for r in range(z.block_rows):
                full_row = p * z.block_rows + r
                line = mask_ref[full_row : full_row + 1, c * LANES : (c + 1) * LANES]
                wet = jnp.where(sub == c * z.block_rows + r, line.astype(F32), wet)
        wet_ref[p] = wet
        wets.append(wet)
    for b in range(z.batches):
        near = jnp.int32(0)
        tile = lax.rem(owner[b], z.groups_d) * z.cols
        first_row = owner[b] // z.groups_d * z.block_rows
        for i in range(z.batch):
            k = b * z.batch + i
            at_row = first_row + index[b, 2, i]
            at_col = tile + index[b, 3, i]
            rows_s = jnp.where(row == k, at_row, rows_s)
            cols_s = jnp.where(row == k, at_col, cols_s)
            rows_l = jnp.where(lane == k, at_row, rows_l)
            cols_l = jnp.where(lane == k, at_col, cols_l)
            ahead = lax.rem(at_col - first_col + z.width, z.width)
            behind = z.width - ahead
            reach = 2 * LOC_RADIUS
            close = (ahead < z.cols + reach) | (behind < reach)
            near = jnp.where(close, 1, near)
        flag[b] = near

        @pl.when(near > 0)
        def _():
            for i in range(z.batch):
                k = b * z.batch + i
                at_row = first_row + index[b, 2, i]
                at_col = tile + index[b, 3, i]
                for p in range(z.groups_m):
                    rho = taper(cell_row + (p * z.block_rows - at_row), cell_col - at_col, z.width)
                    taper_ref[p, k] = wets[p] * rho
    mutual_ref[...] = taper(rows_s - rows_l, cols_s - cols_l, z.width)


def filter_kernel(
    z, value, error, got_ref, mutual_ref,
    gain_ref, part_ref, cross_ref, lift_ref, relay_ref, gap_ref,
):
    n = z.obs
    eight = z.groups_m * SUBS
    stacked = []
    for x in range(z.groups_m):
        total = got_ref[0, x]
        for d in range(1, z.groups_d):
            total = total + got_ref[d, x]
        stacked.append(total)
    stacked = jnp.concatenate(stacked, axis=0)
    square = (n, LANES)
    prior = jnp.zeros(square, F32)
    row, lane = iota(square, 0), iota(square, 1)
    for v in range(z.window // SUBS):
        pick = (lane == row + v * n).astype(F32)
        part = dot_exact(pick, stacked, (1, 1))
        src = iota((eight, LANES), 0)
        dst = iota((eight, LANES), 1)
        slot = v * SUBS + src % SUBS
        place_of = jnp.where(slot < z.own, (src // SUBS) * z.own + slot, -1)
        prior = prior + dot_exact(part, (dst == place_of).astype(F32), (1, 0))
    mean = jnp.sum(prior, axis=1, keepdims=True) * (1.0 / z.members)
    anomaly = jnp.where(lane < z.members, prior - mean, 0.0)
    values = jnp.zeros(square, F32)
    for k in range(n):
        values = jnp.where(row == k, value[k // z.batch, k % z.batch], values)
    gap_ref[...] = values - mean
    mutual = mutual_ref[...]
    relay = jnp.zeros(square, F32)
    inverse_l = jnp.zeros(square, F32)
    inverse_s = jnp.zeros(square, F32)
    shrink_s = jnp.zeros(square, F32)
    spread = float(z.members - 1)
    for k in range(n):
        b, i = divmod(k, z.batch)
        own = anomaly[k : k + 1, :]
        product = jnp.sum(anomaly * own, axis=1, keepdims=True)
        variance = product[k : k + 1, :] * (1.0 / spread) + error[b, i]
        inverse = 1.0 / (spread * variance)
        shrink = 1.0 / (1.0 + jnp.sqrt(error[b, i] / variance))
        ratio = jnp.where(row[:, 0:1] > k, mutual[:, k : k + 1] * product * inverse, 0.0)
        anomaly = anomaly - (shrink * ratio) * own
        relay = jnp.where(lane == k, ratio, relay)
        inverse_l = jnp.where(lane == k, inverse, inverse_l)
        inverse_s = jnp.where(row == k, inverse, inverse_s)
        shrink_s = jnp.where(row == k, shrink, shrink_s)
    gram = dot_exact(anomaly, anomaly, (1, 1))
    cross_ref[...] = -shrink_s[:, 0:n] * inverse_l[:, 0:n] * gram
    high, low = split(anomaly * inverse_s)

    def tripled(count, offset, width):
        shape = (LANES, 3 * width)
        src, dst = iota(shape, 0), iota(shape, 1)
        third, slot = dst // width, dst % width - offset
        hit = (src == slot) & (slot >= 0) & (slot < count)
        upper = (hit & (third < 2)).astype(BF16)
        lower = (hit & (third == 2)).astype(BF16)
        return (dot(high, upper) + dot(low, lower)).astype(BF16)

    gain_ref[...] = tripled(z.members, 0, z.members)
    made = {}
    for p in range(z.groups_m):
        offset = p * z.own - z.start(p)
        if offset not in made:
            made[offset] = tripled(z.own, offset, z.window)
        part_ref[p] = made[offset]
    eye = (iota((z.members, LANES), 0) == iota((z.members, LANES), 1)).astype(F32)
    lift_ref[...] = dot_exact(eye, shrink_s * anomaly, (1, 1))
    relay_ref[...] = relay


def stacked_rows(flat, first, count, lines):
    x = [flat[pl.ds(first + t, count, stride=lines), :] for t in range(2)]
    x = jnp.concatenate(x, axis=1)
    high = x.astype(BF16).astype(F32)
    return jnp.concatenate([high, x - high, high], axis=0).astype(BF16)


def solve_gains(z, flag, cross, taper_of, work, gains):
    n, size = z.obs, z.batch
    every = range(z.groups)

    for b in range(z.batches):

        @pl.when(flag[b] > 0)
        def _():
            part = [
                [work[pl.ds(g * SUBS * n + b * size + i, SUBS, stride=n), :] for g in every]
                for i in range(size)
            ]
            for before in range(b):

                def add(part):
                    part = [list(each) for each in part]
                    for j in range(before * size, (before + 1) * size):
                        held = [gains[g * n + j] for g in every]
                        for i in range(size):
                            factor = cross[j, b * size + i]
                            for g in every:
                                part[i][g] = part[i][g] + factor * held[g]
                    return part

                part = lax.cond(flag[before] > 0, add, lambda part: part, part)
            for i in range(size):
                k = b * size + i
                rho = taper_of(k)
                for g in every:
                    kalman = rho * part[i][g]
                    gains[g * n + k] = kalman
                    for j in range(i + 1, size):
                        part[j][g] = part[j][g] + cross[k, b * size + j] * kalman

        @pl.when(flag[b] == 0)
        def _():
            for i in range(size):
                for g in every:
                    gains[g * n + b * size + i] = jnp.zeros((SUBS, LANES), F32)


def sums_kernel(
    z, group, cross, flag, x_ref, part_ref, taper_ref, wet_ref, sums_ref, work, gains, total, held
):
    n = z.obs
    step = pl.program_id(0)
    lines = z.lines
    flat = x_ref.reshape(z.members * lines, LANES)
    first_line = pl.multiple_of(step * (z.groups * SUBS), SUBS)
    total[...] = jnp.zeros_like(total)
    every = range(z.groups)

    for p in range(z.groups_m):
        for g in every:
            for s in range(0, SUBS, 2):
                first = first_line + z.start(p) * lines + g * SUBS + s
                x = stacked_rows(flat, first, z.window, lines)
                got = dot(part_ref[p], x)
                at = (g * SUBS + s) * n
                work[at : at + n, :] = got[:, 0:LANES]
                work[at + n : at + 2 * n, :] = got[:, LANES : 2 * LANES]
        solve_gains(z, flag, cross, lambda k: taper_ref[p, k], work, gains)
        for g in every:
            for k in range(n):
                total[g * n + k] = total[g * n + k] + gains[g * n + k]
    for g in every:
        for k in range(n):
            work[pl.ds(g * SUBS * n + k, SUBS, stride=n), :] = total[g * n + k]
        for q in range(z.per_step):
            first = g * SUBS + q * z.cells
            each = work[first * n : (first + 1) * n, :]
            for s in range(first + 1, first + z.cells):
                each = each + work[s * n : (s + 1) * n, :]
            fl = (step * z.groups + g) * z.per_step + q
            held[pl.ds(pl.multiple_of(fl * n, n), n), :] = each

    @pl.when(step == z.steps // z.groups - 1)
    def _():
        ones = jnp.ones((SUBS, LANES), F32)
        wet = jnp.sum(wet_ref[group[0]][0 : z.cells, :], axis=0, keepdims=True)
        rows = [
            dot_exact(ones, held[i * LANES : (i + 1) * LANES, :], (1, 1))[0:1, :]
            for i in range(z.sum_rows)
        ]
        rows.append(wet)
        for d in range(z.groups_d):
            for i, line in enumerate(rows):
                sums_ref[d, i : i + 1, :] = line


def weights_kernel(z, index, *refs):
    lift_ref, relay_ref, gap_ref, weight_ref, shift_ref = refs[z.groups_m :]
    n = z.obs
    sums = sum(ref[d] for ref in refs[: z.groups_m] for d in range(z.groups_d))
    count = jnp.sum(sums[z.sum_rows : z.sum_rows + 1, :], axis=1, keepdims=True)
    lines = []
    for fl in range(z.states):
        i, c = divmod(fl, z.pack_states)
        lines.append(sums[i : i + 1, c * n : (c + 1) * n])
    pad = -z.states % SUBS
    table = jnp.concatenate(lines + [jnp.zeros((pad, n), F32)], axis=0) / count
    shape = (n, z.states + pad)
    row, fl_lane = iota(shape, 0), iota(shape, 1)
    at = jnp.zeros(shape, jnp.int32)
    for k in range(n):
        b, i = divmod(k, z.batch)
        at = jnp.where(row == k, index[b, 0, i] * z.levels + index[b, 1, i], at)
    chosen = dot_exact((fl_lane == at).astype(F32), table, (1, 0))
    later = iota((n, n), 0) // z.batch > iota((n, n), 1) // z.batch
    relay = relay_ref[:, 0:n] - jnp.where(later, chosen, 0.0)
    gap = gap_ref[...]
    for k in range(n):
        gap = gap - relay[:, k : k + 1] * gap[k : k + 1, :]
    diagonal = iota((n, n), 0) == iota((n, n), 1)
    gap = jnp.sum(jnp.where(diagonal, gap[:, 0:n], 0.0), axis=0, keepdims=True)
    shift = jnp.sum(table * gap, axis=1, keepdims=True)
    shift_ref[...] = jnp.broadcast_to(shift, shift_ref.shape)
    high, low = split(gap - lift_ref[...])
    src, dst = iota((n, 3 * n), 0), iota((n, 3 * n), 1)
    hit = src == dst % n
    upper = (hit & (dst < 2 * n)).astype(BF16)
    lower = (hit & (dst >= 2 * n)).astype(BF16)
    weight_ref[...] = (dot(high, upper) + dot(low, lower)).astype(BF16)


def update_kernel(z, group, cross, flag, *refs):
    n = z.obs
    slabs = refs[: z.groups_m]
    gain_ref, taper_ref, wet_ref, weight_ref, shift_ref, out_ref = refs[z.groups_m : -5]
    got, made, work, gains, out_sems = refs[-5:]
    chunk = z.groups * SUBS
    flat_x = got.reshape(z.members * chunk, LANES)
    flat_o = made.reshape(z.members * z.lines, LANES)
    size = z.members * chunk
    every = range(z.groups)

    def lines(at):
        return pl.ds(pl.multiple_of(at * chunk, SUBS), chunk)

    def stores(at):
        for x in range(z.groups_m):
            first = jnp.bitwise_xor(group[0], x) * z.own
            here = made.at[at, x * z.own : (x + 1) * z.own]
            there = out_ref.at[pl.ds(first, z.own), lines(at)]
            yield pltpu.make_async_copy(here, there, out_sems.at[x, at])

    count = z.steps // z.groups
    wet = wet_ref[group[0]]

    def advance(at, carry):
        for x, slab in enumerate(slabs):
            src = slab.at[group[0]] if x == 0 else slab
            got[x * z.own : (x + 1) * z.own] = src[:, lines(at)]
        base = pl.multiple_of(at * size, SUBS)
        for g in every:
            for s in range(0, SUBS, 2):
                x = stacked_rows(flat_x, g * SUBS + s, z.members, chunk)
                new = dot(gain_ref[...], x)
                line = (g * SUBS + s) * n
                work[line : line + n, :] = new[:, 0:LANES]
                work[line + n : line + 2 * n, :] = new[:, LANES : 2 * LANES]
        solve_gains(z, flag, cross, lambda k: taper_ref[group[0], k], work, gains)
        for g in every:
            for k in range(n):
                work[pl.ds(g * SUBS * n + k, SUBS, stride=n), :] = gains[g * n + k]
            for s in range(0, SUBS, 2):
                line = (g * SUBS + s) * n
                k = [work[line : line + n, :], work[line + n : line + 2 * n, :]]
                k = jnp.concatenate(k, axis=1)
                high = k.astype(BF16)
                low = (k - high.astype(F32)).astype(BF16)
                total = dot(weight_ref[...], jnp.concatenate([high, low, high], axis=0))
                for t in range(2):
                    fl = (at * z.groups + g) * z.per_step + (s + t) // z.cells
                    off = shift_ref[pl.ds(fl, 1), :] * wet[s + t : s + t + 1, :]
                    line = g * SUBS + s + t
                    old = flat_x[pl.ds(line, z.members, stride=chunk), :]
                    new = old + (total[:, t * LANES : (t + 1) * LANES] - off)
                    flat_o[pl.ds(base + line, z.members, stride=chunk), :] = new
        for copy in stores(at):
            copy.start()
        return carry

    lax.fori_loop(0, count, advance, 0)

    def drain(at, carry):
        for copy in stores(at):
            copy.wait()
        return carry

    lax.fori_loop(0, count, drain, 0)


def whole(*shape):
    return pl.BlockSpec(shape, lambda *_: (0,) * len(shape))


def smem():
    return pl.BlockSpec(memory_space=SMEM)


def struct(*shape, dtype=F32):
    return jax.ShapeDtypeStruct(shape, dtype)


def grant(mebibytes):
    return pltpu.CompilerParams(vmem_limit_bytes=mebibytes << 20)


def exchange(copies):
    return lax.all_to_all(copies, "domain", 0, 0, tiled=True)


def swap(z, array, x):
    return lax.ppermute(array, "member", [(p, p ^ x) for p in range(z.groups_m)])


def local(ensemble, velocity, diffusivity, land_mask, obs_index, obs_owner, obs_value, obs_error):
    z = Sizes(ensemble, obs_index)
    group = lax.axis_index("member").reshape(1)
    domain = lax.axis_index("domain").reshape(1)
    index = jnp.swapaxes(obs_index, 1, 2)
    state = ensemble.reshape(z.own, z.states, z.rows, z.cols)
    vmem = pl.BlockSpec(memory_space=VMEM)
    state = pltpu.with_memory_space_constraint(state, pltpu.HBM)
    side = pl.BlockSpec((z.rows, LANES), lambda i: (0, i))
    halo = z.parts * LANES
    hbm = pl.BlockSpec(memory_space=pl.ANY)
    arrived = [VMEM(state.shape, F32), pltpu.SemaphoreType.DMA((z.parts,))]
    first, last = pl.pallas_call(
        functools.partial(edges_kernel, z),
        grid=(z.parts,),
        in_specs=[hbm],
        out_specs=[side] * 2,
        out_shape=[struct(z.rows, halo)] * 2,
        scratch_shapes=arrived,
        name="edges",
        compiler_params=grant(12),
    )(state)
    up = [(i, (i + 1) % z.groups_d) for i in range(z.groups_d)]
    down = [(j, i) for i, j in up]
    before = lax.ppermute(last, "domain", up)
    after = lax.ppermute(first, "domain", down)
    n = z.obs
    tapers, wet, mutual, flag = pl.pallas_call(
        functools.partial(tapers_kernel, z),
        in_specs=[smem()] * 3 + [vmem],
        out_specs=[vmem] * 3 + [smem()],
        out_shape=[
            struct(z.groups_m, n, SUBS, LANES),
            struct(z.groups_m, SUBS, LANES),
            struct(n, LANES),
            struct(z.batches, dtype=jnp.int32),
        ],
        name="tapers",
        compiler_params=grant(8),
    )(domain, index, obs_owner, land_mask)
    slots = range(1, z.groups_m)
    stepped, *moved, own_priors = pl.pallas_call(
        functools.partial(forecast_kernel, z),
        grid=(z.parts,),
        in_specs=[smem()] * 5
        + [
            hbm,
            whole(z.rows, halo),
            whole(z.rows, halo),
            whole(*velocity.shape),
            whole(*land_mask.shape),
        ],
        out_specs=[vmem] * z.groups_m + [whole(SUBS, LANES)],
        out_shape=[struct(z.groups_m, z.own, z.lines, LANES)]
        + [struct(z.own, z.lines, LANES) for _ in slots]
        + [struct(SUBS, LANES)],
        scratch_shapes=[
            VMEM((z.window, LANES), F32),
        ]
        + arrived,
        name="forecast",
        compiler_params=grant(20),
    )(group, domain, index, obs_owner, diffusivity, state, before, after, velocity, land_mask)
    priors = [own_priors] + [swap(z, own_priors, x) for x in slots]
    moved = [swap(z, slab, x) for x, slab in zip(slots, moved)]
    priors = jnp.broadcast_to(jnp.stack(priors)[None], (z.groups_d, z.groups_m, SUBS, LANES))
    priors = exchange(priors)
    gain, part, cross, lift, relay, gap = pl.pallas_call(
        functools.partial(filter_kernel, z),
        in_specs=[smem()] * 2 + [vmem] * 2,
        out_specs=[vmem] * 6,
        out_shape=[
            struct(n, 3 * z.members, dtype=BF16),
            struct(z.groups_m, n, 3 * z.window, dtype=BF16),
            struct(n, n),
            struct(z.members, n),
            struct(n, LANES),
            struct(n, LANES),
        ],
        name="filter",
        compiler_params=grant(8),
    )(obs_value, obs_error, priors, mutual)
    lines = z.groups * SUBS
    grid = (z.steps // z.groups,)
    work = VMEM((z.groups * SUBS * n, LANES), F32)
    gains = VMEM((z.groups * n, SUBS, LANES), F32)
    sums = pl.pallas_call(
        functools.partial(sums_kernel, z),
        grid=grid,
        in_specs=[
            smem(),
            smem(),
            smem(),
            vmem,
            vmem,
            vmem,
            vmem,
        ],
        out_specs=whole(z.groups_d, z.sum_rows + 1, LANES),
        out_shape=struct(z.groups_d, z.sum_rows + 1, LANES),
        scratch_shapes=[work, gains, gains, VMEM((z.sum_rows * LANES, LANES), F32)],
        name="sums",
        compiler_params=grant(12),
    )(group, cross, flag, stepped.reshape(z.members, z.lines, LANES), part, tapers, wet)
    sums = exchange(sums)
    sums = [sums] + [swap(z, sums, x) for x in slots]
    padded = z.states + -z.states % SUBS
    weight, shift = pl.pallas_call(
        functools.partial(weights_kernel, z),
        in_specs=[smem()] + [vmem] * (z.groups_m + 3),
        out_specs=[vmem] * 2,
        out_shape=[struct(z.members, 3 * n, dtype=BF16), struct(padded, LANES)],
        name="weights",
        compiler_params=grant(8),
    )(index, *sums, lift, relay, gap)
    sems = pltpu.SemaphoreType.DMA((z.groups_m, z.steps // z.groups))
    result = pl.pallas_call(
        functools.partial(update_kernel, z),
        in_specs=[smem()] * 3 + [vmem] * (z.groups_m + 5),
        out_specs=hbm,
        out_shape=struct(z.members, z.lines, LANES),
        scratch_shapes=[
            VMEM((z.members, lines, LANES), F32),
            VMEM((z.steps // z.groups, z.members, lines, LANES), F32),
            work,
            gains,
            sems,
        ],
        name="update",
        compiler_params=grant(20),
    )(group, cross, flag, stepped, *moved, gain, tapers, wet, weight, shift)
    result = result.reshape(z.members, z.fields, z.levels, z.col_tiles, z.block_rows, LANES)
    result = jnp.swapaxes(result, 3, 4)
    return result.reshape(z.members, z.fields, z.levels, z.block_rows, z.cols)


def solution(mesh):
    in_specs = (
        P("member", None, None, None, "domain"),
        P(None, None, None, "domain"),
        P(),
        P(None, "domain"),
        P(),
        P(),
        P(),
        P(),
    )
    out_specs = P(None, None, None, "member", "domain")
    return jax.shard_map(local, mesh=mesh, in_specs=in_specs, out_specs=out_specs, check_vma=False)
```

```python
import functools

import jax
import jax.numpy as jnp
from jax import lax
from jax.experimental import pallas as pl
from jax.experimental.pallas import tpu as pltpu
from jax.sharding import PartitionSpec as P


LOC_RADIUS = 64
LANES = 128
SUBS = 8
F32 = jnp.float32
BF16 = jnp.bfloat16
HIGHEST = lax.Precision.HIGHEST
VMEM = pltpu.VMEM
SMEM = pltpu.SMEM


def gaspari(scaled):
    scaled_safe = jnp.maximum(scaled, 1.0)
    near_part = (
        ((-0.25 * scaled + 0.5) * scaled + 0.625) * scaled - 5.0 / 3.0
    ) * scaled * scaled + 1.0
    far_part = (
        ((((scaled / 12.0 - 0.5) * scaled + 0.625) * scaled + 5.0 / 3.0) * scaled - 5.0) * scaled
        + 4.0
        - 2.0 / (3.0 * scaled_safe)
    )
    return jnp.where(scaled <= 1.0, near_part, jnp.where(scaled < 2.0, far_part, 0.0))


def taper(row_gap, col_gap, grid_width):
    col_gap = jnp.abs(col_gap)
    col_gap = jnp.minimum(col_gap, grid_width - col_gap)
    square = (col_gap * col_gap + row_gap * row_gap).astype(F32)
    return gaspari(jnp.sqrt(square) * (1.0 / LOC_RADIUS))


def iota(shape, dim):
    return lax.broadcasted_iota(jnp.int32, shape, dim)


def split(value):
    high = value.astype(BF16)
    return high, (value - high.astype(F32)).astype(BF16)


def dot(a, b):
    return lax.dot_general(a, b, (((1,), (0,)), ((), ())), preferred_element_type=F32)


def dot_exact(a, b, dims):
    return lax.dot_general(
        a, b, ((dims[:1], dims[1:]), ((), ())), precision=HIGHEST, preferred_element_type=F32
    )


class Sizes:
    def __init__(self, ensemble, obs_index):
        self.own, self.fields, self.levels, self.rows, self.cols = ensemble.shape
        self.states = self.fields * self.levels
        self.groups_m = lax.axis_size("member")
        self.groups_d = lax.axis_size("domain")
        self.members = self.own * self.groups_m
        self.block_rows = self.rows // self.groups_m
        self.col_tiles = self.cols // LANES
        self.cells = self.block_rows * self.col_tiles
        self.deep = SUBS // self.block_rows
        self.width = self.cols * self.groups_d
        self.batches, self.batch = obs_index.shape[:2]
        self.obs = self.batches * self.batch
        self.pack_states = LANES // self.obs
        self.sum_rows = -(-self.states // self.pack_states)
        self.part = next(m for m in (5, 4, 3, 2, 1) if self.own % m == 0)
        self.parts = self.own // self.part
        self.lines = self.states * self.cells
        stacks = self.states // self.deep
        self.groups = next(g for g in (3, 2, 1) if stacks % g == 0)
        self.chunks = stacks // self.groups
        self.chunk_states = self.deep * self.groups
        self.chunk_lines = self.chunk_states * self.cells
        self.window = -(-self.own // SUBS) * SUBS
        self.pitch = self.lines + SUBS * (1 - self.lines // SUBS % 2)
        self.chunk_pitch = self.chunk_lines + SUBS * (1 - self.chunk_lines // SUBS % 2)

    def line(self, g, s, c):
        q, r = divmod(s, self.block_rows)
        return (g * self.deep + q) * self.cells + c * self.block_rows + r

    def start(self, p):
        return min(p * self.own, self.members - self.window)


def arrivals(z, step, given, source, sems):
    def copy(at):
        part = pl.ds(at * z.part, z.part)
        return pltpu.make_async_copy(given.at[part], source.at[part], sems.at[at])

    @pl.when(step == 0)
    def _():
        for at in range(z.parts):
            copy(at).start()

    copy(step).wait()


def edges_kernel(z, given, first_ref, last_ref, source, sems):
    step = pl.program_id(0)
    arrivals(z, step, given, source, sems)
    lane = iota((z.rows, LANES), 1)
    first = jnp.zeros((z.rows, LANES), F32)
    last = first
    for m in range(z.part):
        for fl in range(z.states):
            hit = lane == m * z.states + fl
            at = step * z.part + m
            first = jnp.where(hit, source[at, fl, :, 0:1], first)
            last = jnp.where(hit, source[at, fl, :, z.cols - 1 : z.cols], last)
    first_ref[...] = first
    last_ref[...] = last


def forecast_kernel(
    z, group, domain, index, owner, diff, given, before_ref, after_ref, vel_ref, mask_ref,
    state, *refs,
):
    others = refs[: z.groups_m - 1]
    obs_ref, picked, source, in_sems = refs[z.groups_m - 1 :]
    step = pl.program_id(0)
    arrivals(z, step, given, source, in_sems)
    shape = (z.rows, z.cols)
    row, col = iota(shape, 0), iota(shape, 1)
    wet = mask_ref[...].astype(F32)
    flat = state.reshape(z.members * z.pitch, LANES)
    member = pl.multiple_of(step * (z.part * z.pitch), SUBS)
    side = pl.ds(pl.multiple_of(step * LANES, LANES), LANES)
    before = before_ref[:, side]
    after = after_ref[:, side]
    for fl in range(z.states):
        level = fl % z.levels
        spread = diff[fl // z.levels]
        half_u = 0.5 * vel_ref[0, level]
        half_v = 0.5 * vel_ref[1, level]
        center = wet * (1.0 - 4.0 * spread)
        east = wet * (spread - half_u)
        west = wet * (spread + half_u)
        north = jnp.where(row == z.rows - 1, 0.0, wet * (spread - half_v))
        south = jnp.where(row == 0, 0.0, wet * (spread + half_v))
        for m in range(z.part):
            x = source[step * z.part + m, fl]
            at = m * z.states + fl
            nxt = jnp.where(col == z.cols - 1, after[:, at : at + 1], pltpu.roll(x, z.cols - 1, 1))
            prv = jnp.where(col == 0, before[:, at : at + 1], pltpu.roll(x, 1, 1))
            y = (
                center * x
                + east * nxt
                + west * prv
                + north * pltpu.roll(x, z.rows - 1, 0)
                + south * pltpu.roll(x, 1, 0)
            )
            for p in range(z.groups_m):
                for c in range(z.col_tiles):
                    line = (p * z.own + m) * z.pitch + fl * z.cells + c * z.block_rows
                    flat[pl.ds(member + line, z.block_rows), :] = y[
                        p * z.block_rows : (p + 1) * z.block_rows, c * LANES : (c + 1) * LANES
                    ]

    part = pl.ds(step * z.part, z.part)
    for x, other in enumerate(others, 1):
        other[part] = state[jnp.bitwise_xor(group[0], x), part, 0 : z.lines]

    @pl.when(step == z.parts - 1)
    def _():
        picked[...] = jnp.zeros_like(picked)
        lane, slot = iota((z.window, LANES), 1), iota((z.window, LANES), 0)
        for b in range(z.batches):

            @pl.when(lax.rem(owner[b], z.groups_d) == domain[0])
            def _():
                total = jnp.zeros((z.window, LANES), F32)
                own = owner[b] // z.groups_d * z.own
                first = jnp.minimum(own, z.members - z.window)
                for i in range(z.batch):
                    fl = index[b, 0, i] * z.levels + index[b, 1, i]
                    at = index[b, 3, i]
                    cell = (at // LANES) * z.block_rows + index[b, 2, i]
                    line = first * z.pitch + fl * z.cells + cell
                    got = flat[pl.ds(line, z.window, stride=z.pitch), :]
                    at = lax.rem(at, LANES)
                    got = jnp.where(lane == at, got, 0.0)
                    turn = lax.rem(b * z.batch + i + LANES - at, LANES)
                    total = total + pltpu.roll(got, turn, 1)
                total = pltpu.roll(total, lax.rem(first + z.window - own, z.window), 0)
                picked[...] = picked[...] + jnp.where(slot < z.own, total, 0.0)

        total = picked[0:SUBS, :]
        for v in range(1, z.window // SUBS):
            total = total + pltpu.roll(picked[v * SUBS : (v + 1) * SUBS, :], v * z.obs, 1)
        obs_ref[...] = total


def tapers_kernel(z, domain, index, owner, mask_ref, taper_ref, wet_ref, mutual_ref, flag):
    n = z.obs
    square = (n, LANES)
    row, lane = iota(square, 0), iota(square, 1)
    rows_s, cols_s = jnp.zeros(square, jnp.int32), jnp.zeros(square, jnp.int32)
    rows_l, cols_l = rows_s, cols_s
    shape = (SUBS, LANES)
    cell_row = iota(shape, 0) % z.block_rows
    first_col = domain[0] * z.cols
    wets = {}
    for p in range(z.groups_m):
        for c in range(z.col_tiles):
            wet = jnp.zeros(shape, F32)
            for r in range(z.block_rows):
                full_row = p * z.block_rows + r
                line = mask_ref[full_row : full_row + 1, c * LANES : (c + 1) * LANES]
                wet = jnp.where(cell_row == r, line.astype(F32), wet)
            wet_ref[p, c] = wet
            wets[p, c] = wet
    for b in range(z.batches):
        tile = lax.rem(owner[b], z.groups_d) * z.cols
        first_row = owner[b] // z.groups_d * z.block_rows
        for i in range(z.batch):
            k = b * z.batch + i
            at_row = first_row + index[b, 2, i]
            at_col = tile + index[b, 3, i]
            rows_s = jnp.where(row == k, at_row, rows_s)
            cols_s = jnp.where(row == k, at_col, cols_s)
            rows_l = jnp.where(lane == k, at_row, rows_l)
            cols_l = jnp.where(lane == k, at_col, cols_l)
        for c in range(z.col_tiles):
            near = jnp.int32(0)
            start = first_col + c * LANES
            reach = 2 * LOC_RADIUS
            for i in range(z.batch):
                ahead = lax.rem(tile + index[b, 3, i] - start + z.width, z.width)
                close = (ahead < LANES + reach) | (z.width - ahead < reach)
                near = jnp.where(close, 1, near)
            flag[b, c] = near

            @pl.when(near > 0)
            def _():
                cell_col = start + iota(shape, 1)
                for i in range(z.batch):
                    at_row = first_row + index[b, 2, i]
                    at_col = tile + index[b, 3, i]
                    for p in range(z.groups_m):
                        row_gap = cell_row + (p * z.block_rows - at_row)
                        rho = taper(row_gap, cell_col - at_col, z.width)
                        taper_ref[p, c, b * z.batch + i] = wets[p, c] * rho

    mutual_ref[...] = taper(rows_s - rows_l, cols_s - cols_l, z.width)


def filter_kernel(
    z, value, error, got_ref, mutual_ref,
    gain_ref, part_ref, cross_ref, lift_ref, relay_ref, gap_ref,
):
    n = z.obs
    eight = z.groups_m * SUBS
    stacked = []
    for x in range(z.groups_m):
        total = got_ref[0, x]
        for d in range(1, z.groups_d):
            total = total + got_ref[d, x]
        stacked.append(total)
    stacked = jnp.concatenate(stacked, axis=0)
    square = (n, LANES)
    prior = jnp.zeros(square, F32)
    row, lane = iota(square, 0), iota(square, 1)
    for v in range(z.window // SUBS):
        pick = (lane == row + v * n).astype(F32)
        part = dot_exact(pick, stacked, (1, 1))
        src = iota((eight, LANES), 0)
        dst = iota((eight, LANES), 1)
        slot = v * SUBS + src % SUBS
        place_of = jnp.where(slot < z.own, (src // SUBS) * z.own + slot, -1)
        prior = prior + dot_exact(part, (dst == place_of).astype(F32), (1, 0))
    mean = jnp.sum(prior, axis=1, keepdims=True) * (1.0 / z.members)
    anomaly = jnp.where(lane < z.members, prior - mean, 0.0)
    values = jnp.zeros(square, F32)
    for k in range(n):
        values = jnp.where(row == k, value[k // z.batch, k % z.batch], values)
    gap_ref[...] = values - mean
    mutual = mutual_ref[...]
    relay = jnp.zeros(square, F32)
    inverse_l = jnp.zeros(square, F32)
    inverse_s = jnp.zeros(square, F32)
    shrink_s = jnp.zeros(square, F32)
    spread = float(z.members - 1)
    for k in range(n):
        b, i = divmod(k, z.batch)
        own = anomaly[k : k + 1, :]
        product = jnp.sum(anomaly * own, axis=1, keepdims=True)
        variance = product[k : k + 1, :] * (1.0 / spread) + error[b, i]
        inverse = 1.0 / (spread * variance)
        shrink = 1.0 / (1.0 + jnp.sqrt(error[b, i] / variance))
        ratio = jnp.where(row[:, 0:1] > k, mutual[:, k : k + 1] * product * inverse, 0.0)
        anomaly = anomaly - (shrink * ratio) * own
        relay = jnp.where(lane == k, ratio, relay)
        inverse_l = jnp.where(lane == k, inverse, inverse_l)
        inverse_s = jnp.where(row == k, inverse, inverse_s)
        shrink_s = jnp.where(row == k, shrink, shrink_s)
    gram = dot_exact(anomaly, anomaly, (1, 1))
    cross_ref[...] = -shrink_s[:, 0:n] * inverse_l[:, 0:n] * gram
    high, low = split(anomaly * inverse_s)

    def tripled(count, offset, width):
        shape = (LANES, 3 * width)
        src, dst = iota(shape, 0), iota(shape, 1)
        third, slot = dst // width, dst % width - offset
        hit = (src == slot) & (slot >= 0) & (slot < count)
        upper = (hit & (third < 2)).astype(BF16)
        lower = (hit & (third == 2)).astype(BF16)
        return (dot(high, upper) + dot(low, lower)).astype(BF16)

    gain_ref[...] = tripled(z.members, 0, z.members)
    made = {}
    for p in range(z.groups_m):
        offset = p * z.own - z.start(p)
        if offset not in made:
            made[offset] = tripled(z.own, offset, z.window)
        part_ref[p] = made[offset]
    eye = (iota((z.members, LANES), 0) == iota((z.members, LANES), 1)).astype(F32)
    lift_ref[...] = dot_exact(eye, shrink_s * anomaly, (1, 1))
    relay_ref[...] = relay


def stacked_rows(flat, first, count, lines):
    x = [flat[pl.ds(first + t, count, stride=lines), :] for t in range(2)]
    x = jnp.concatenate(x, axis=1)
    high = x.astype(BF16).astype(F32)
    return jnp.concatenate([high, x - high, high], axis=0).astype(BF16)


def solve_gains(z, active, cross, taper_of, work, gains, total=None):
    n, size = z.obs, z.batch
    every = range(z.groups)

    for b in range(z.batches):

        @pl.when(active(b))
        def _():
            part = [
                [work[pl.ds(g * SUBS * n + b * size + i, SUBS, stride=n), :] for g in every]
                for i in range(size)
            ]
            for before in range(b):

                def add(part):
                    part = [list(each) for each in part]
                    for j in range(before * size, (before + 1) * size):
                        held = [gains[g * n + j] for g in every]
                        for i in range(size):
                            factor = cross[j, b * size + i]
                            for g in every:
                                part[i][g] = part[i][g] + factor * held[g]
                    return part

                part = lax.cond(active(before), add, lambda part: part, part)
            for i in range(size):
                k = b * size + i
                rho = taper_of(k)
                for g in every:
                    kalman = rho * part[i][g]
                    gains[g * n + k] = kalman
                    if total is not None:
                        total[g * n + k] = total[g * n + k] + kalman
                    for j in range(i + 1, size):
                        part[j][g] = part[j][g] + cross[k, b * size + j] * kalman

        if total is None:

            @pl.when(jnp.logical_not(active(b)))
            def _():
                for i in range(size):
                    for g in every:
                        gains[g * n + b * size + i] = jnp.zeros((SUBS, LANES), F32)


def project(z, flat, first, count, stride, c, left, work):
    n = z.obs
    for g in range(z.groups):
        for s in range(0, SUBS, 2):
            x = stacked_rows(flat, first + z.line(g, s, c), count, stride)
            got = dot(left, x)
            at = (g * SUBS + s) * n
            work[at : at + n, :] = got[:, 0:LANES]
            work[at + n : at + 2 * n, :] = got[:, LANES : 2 * LANES]


def sums_kernel(
    z, group, cross, flag, x_ref, part_ref, taper_ref, wet_ref, sums_ref, work, gains, total, held
):
    n = z.obs
    step = pl.program_id(0)
    chunk, c = step // z.col_tiles, lax.rem(step, z.col_tiles)
    flat = x_ref.reshape(z.members * z.pitch, LANES)
    first_line = pl.multiple_of(chunk * z.chunk_lines, SUBS)
    total[...] = jnp.zeros_like(total)
    every = range(z.groups)

    @pl.when(step == 0)
    def _():
        held[...] = jnp.zeros_like(held)

    for p in range(z.groups_m):
        first = first_line + z.start(p) * z.pitch
        project(z, flat, first, z.window, z.pitch, c, part_ref[p], work)
        solve_gains(
            z, lambda b: flag[b, c] > 0, cross, lambda k: taper_ref[p, c, k], work, gains, total
        )
    for g in every:
        for k in range(n):
            work[pl.ds(g * SUBS * n + k, SUBS, stride=n), :] = total[g * n + k]
        for q in range(z.deep):
            first = g * SUBS + q * z.block_rows
            each = work[first * n : (first + 1) * n, :]
            for s in range(first + 1, first + z.block_rows):
                each = each + work[s * n : (s + 1) * n, :]
            fl = chunk * z.chunk_states + g * z.deep + q
            rows = pl.ds(pl.multiple_of(fl * n, n), n)
            held[rows, :] = held[rows, :] + each

    @pl.when(step == z.chunks * z.col_tiles - 1)
    def _():
        ones = jnp.ones((SUBS, LANES), F32)
        wet = sum(wet_ref[group[0], c] for c in range(z.col_tiles))
        wet = jnp.sum(wet[0 : z.block_rows, :], axis=0, keepdims=True)
        rows = [
            dot_exact(ones, held[i * LANES : (i + 1) * LANES, :], (1, 1))[0:1, :]
            for i in range(z.sum_rows)
        ]
        rows.append(wet)
        for d in range(z.groups_d):
            for i, line in enumerate(rows):
                sums_ref[d, i : i + 1, :] = line


def weights_kernel(z, index, *refs):
    lift_ref, relay_ref, gap_ref, weight_ref, shift_ref = refs[z.groups_m :]
    n = z.obs
    sums = sum(ref[d] for ref in refs[: z.groups_m] for d in range(z.groups_d))
    count = jnp.sum(sums[z.sum_rows : z.sum_rows + 1, :], axis=1, keepdims=True)
    lines = []
    for fl in range(z.states):
        i, c = divmod(fl, z.pack_states)
        lines.append(sums[i : i + 1, c * n : (c + 1) * n])
    pad = -z.states % SUBS
    table = jnp.concatenate(lines + [jnp.zeros((pad, n), F32)], axis=0) / count
    shape = (n, z.states + pad)
    row, fl_lane = iota(shape, 0), iota(shape, 1)
    at = jnp.zeros(shape, jnp.int32)
    for k in range(n):
        b, i = divmod(k, z.batch)
        at = jnp.where(row == k, index[b, 0, i] * z.levels + index[b, 1, i], at)
    chosen = dot_exact((fl_lane == at).astype(F32), table, (1, 0))
    later = iota((n, n), 0) // z.batch > iota((n, n), 1) // z.batch
    relay = relay_ref[:, 0:n] - jnp.where(later, chosen, 0.0)
    gap = gap_ref[...]
    for k in range(n):
        gap = gap - relay[:, k : k + 1] * gap[k : k + 1, :]
    diagonal = iota((n, n), 0) == iota((n, n), 1)
    gap = jnp.sum(jnp.where(diagonal, gap[:, 0:n], 0.0), axis=0, keepdims=True)
    shift = jnp.sum(table * gap, axis=1, keepdims=True)
    shift_ref[...] = jnp.broadcast_to(shift, shift_ref.shape)
    high, low = split(gap - lift_ref[...])
    src, dst = iota((n, 3 * n), 0), iota((n, 3 * n), 1)
    hit = src == dst % n
    upper = (hit & (dst < 2 * n)).astype(BF16)
    lower = (hit & (dst >= 2 * n)).astype(BF16)
    weight_ref[...] = (dot(high, upper) + dot(low, lower)).astype(BF16)


def update_kernel(z, group, cross, flag, *refs):
    n = z.obs
    slabs = refs[: z.groups_m]
    gain_ref, taper_ref, wet_ref, weight_ref, shift_ref, out_ref = refs[z.groups_m : -5]
    got, made, work, gains, out_sems = refs[-5:]
    chunk = z.chunk_lines
    pitch = z.chunk_pitch
    flat_x = got.reshape(z.members * pitch, LANES)
    flat_o = made.reshape(z.chunks * z.members * pitch, LANES)
    size = z.members * pitch

    def lines(at):
        return pl.ds(pl.multiple_of(at * chunk, SUBS), chunk)

    def stores(at, g):
        count = z.deep * z.cells
        begin = g * count
        rows = pl.ds(pl.multiple_of(at * chunk + begin, SUBS), count)
        for x in range(z.groups_m):
            first = jnp.bitwise_xor(group[0], x) * z.own
            here = made.at[at, x * z.own : (x + 1) * z.own, begin : begin + count]
            there = out_ref.at[pl.ds(first, z.own), rows]
            yield pltpu.make_async_copy(here, there, out_sems.at[x, at, g])

    def advance(at, c):
        project(z, flat_x, 0, z.members, pitch, c, gain_ref[...], work)
        own = group[0]
        solve_gains(
            z, lambda b: flag[b, c] > 0, cross, lambda k: taper_ref[own, c, k], work, gains
        )
        wet = wet_ref[own, c]
        base = pl.multiple_of(at * size, SUBS)
        for g in range(z.groups):
            for k in range(n):
                work[pl.ds(g * SUBS * n + k, SUBS, stride=n), :] = gains[g * n + k]
            for s in range(0, SUBS, 2):
                row = (g * SUBS + s) * n
                k = [work[row : row + n, :], work[row + n : row + 2 * n, :]]
                k = jnp.concatenate(k, axis=1)
                high = k.astype(BF16)
                low = (k - high.astype(F32)).astype(BF16)
                total = dot(weight_ref[...], jnp.concatenate([high, low, high], axis=0))
                for t in range(2):
                    fl = at * z.chunk_states + g * z.deep + (s + t) // z.block_rows
                    off = shift_ref[pl.ds(fl, 1), :] * wet[s + t : s + t + 1, :]
                    line = z.line(g, s + t, c)
                    old = flat_x[pl.ds(line, z.members, stride=pitch), :]
                    new = old + (total[:, t * LANES : (t + 1) * LANES] - off)
                    flat_o[pl.ds(base + line, z.members, stride=pitch), :] = new

            @pl.when(c == z.col_tiles - 1)
            def _():
                for copy in stores(at, g):
                    copy.start()

    def advance_chunk(at, carry):
        for x, slab in enumerate(slabs):
            src = slab.at[group[0]] if x == 0 else slab
            got[x * z.own : (x + 1) * z.own, 0:chunk] = src[:, lines(at)]

        def tile(c, carry):
            advance(at, c)
            return carry

        lax.fori_loop(0, z.col_tiles, tile, 0)
        return carry

    lax.fori_loop(0, z.chunks, advance_chunk, 0)

    def drain(at, carry):
        for g in range(z.groups):
            for copy in stores(at, g):
                copy.wait()
        return carry

    lax.fori_loop(0, z.chunks, drain, 0)


def whole(*shape):
    return pl.BlockSpec(shape, lambda *_: (0,) * len(shape))


def smem():
    return pl.BlockSpec(memory_space=SMEM)


def struct(*shape, dtype=F32):
    return jax.ShapeDtypeStruct(shape, dtype)


def grant(mebibytes):
    return pltpu.CompilerParams(vmem_limit_bytes=mebibytes << 20)


def exchange(copies):
    return lax.all_to_all(copies, "domain", 0, 0, tiled=True)


def swap(z, array, x):
    return lax.ppermute(array, "member", [(p, p ^ x) for p in range(z.groups_m)])


def local(ensemble, velocity, diffusivity, land_mask, obs_index, obs_owner, obs_value, obs_error):
    z = Sizes(ensemble, obs_index)
    group = lax.axis_index("member").reshape(1)
    domain = lax.axis_index("domain").reshape(1)
    index = jnp.swapaxes(obs_index, 1, 2)
    state = ensemble.reshape(z.own, z.states, z.rows, z.cols)
    vmem = pl.BlockSpec(memory_space=VMEM)
    state = pltpu.with_memory_space_constraint(state, pltpu.HBM)
    side = pl.BlockSpec((z.rows, LANES), lambda i: (0, i))
    halo = z.parts * LANES
    hbm = pl.BlockSpec(memory_space=pl.ANY)
    arrived = [VMEM(state.shape, F32), pltpu.SemaphoreType.DMA((z.parts,))]
    first, last = pl.pallas_call(
        functools.partial(edges_kernel, z),
        grid=(z.parts,),
        in_specs=[hbm],
        out_specs=[side] * 2,
        out_shape=[struct(z.rows, halo)] * 2,
        scratch_shapes=arrived,
        name="edges",
        compiler_params=grant(12),
    )(state)
    up = [(i, (i + 1) % z.groups_d) for i in range(z.groups_d)]
    down = [(j, i) for i, j in up]
    before = lax.ppermute(last, "domain", up)
    after = lax.ppermute(first, "domain", down)
    n = z.obs
    tapers, wet, mutual, flag = pl.pallas_call(
        functools.partial(tapers_kernel, z),
        in_specs=[smem()] * 3 + [vmem],
        out_specs=[vmem] * 3 + [smem()],
        out_shape=[
            struct(z.groups_m, z.col_tiles, n, SUBS, LANES),
            struct(z.groups_m, z.col_tiles, SUBS, LANES),
            struct(n, LANES),
            struct(z.batches, z.col_tiles, dtype=jnp.int32),
        ],
        name="tapers",
        compiler_params=grant(8),
    )(domain, index, obs_owner, land_mask)
    slots = range(1, z.groups_m)
    stepped, *moved, own_priors = pl.pallas_call(
        functools.partial(forecast_kernel, z),
        grid=(z.parts,),
        in_specs=[smem()] * 5
        + [
            hbm,
            whole(z.rows, halo),
            whole(z.rows, halo),
            whole(*velocity.shape),
            whole(*land_mask.shape),
        ],
        out_specs=[vmem] * z.groups_m + [whole(SUBS, LANES)],
        out_shape=[struct(z.groups_m, z.own, z.pitch, LANES)]
        + [struct(z.own, z.lines, LANES) for _ in slots]
        + [struct(SUBS, LANES)],
        scratch_shapes=[
            VMEM((z.window, LANES), F32),
        ]
        + arrived,
        name="forecast",
        compiler_params=grant(20),
    )(group, domain, index, obs_owner, diffusivity, state, before, after, velocity, land_mask)
    priors = [own_priors] + [swap(z, own_priors, x) for x in slots]
    moved = [swap(z, slab, x) for x, slab in zip(slots, moved)]
    priors = jnp.broadcast_to(jnp.stack(priors)[None], (z.groups_d, z.groups_m, SUBS, LANES))
    priors = exchange(priors)
    gain, part, cross, lift, relay, gap = pl.pallas_call(
        functools.partial(filter_kernel, z),
        in_specs=[smem()] * 2 + [vmem] * 2,
        out_specs=[vmem] * 6,
        out_shape=[
            struct(n, 3 * z.members, dtype=BF16),
            struct(z.groups_m, n, 3 * z.window, dtype=BF16),
            struct(n, n),
            struct(z.members, n),
            struct(n, LANES),
            struct(n, LANES),
        ],
        name="filter",
        compiler_params=grant(8),
    )(obs_value, obs_error, priors, mutual)
    grid = (z.chunks * z.col_tiles,)
    work = VMEM((z.groups * SUBS * n, LANES), F32)
    gains = VMEM((z.groups * n, SUBS, LANES), F32)
    sums = pl.pallas_call(
        functools.partial(sums_kernel, z),
        grid=grid,
        in_specs=[
            smem(),
            smem(),
            smem(),
            vmem,
            vmem,
            vmem,
            vmem,
        ],
        out_specs=whole(z.groups_d, z.sum_rows + 1, LANES),
        out_shape=struct(z.groups_d, z.sum_rows + 1, LANES),
        scratch_shapes=[work, gains, gains, VMEM((z.sum_rows * LANES, LANES), F32)],
        name="sums",
        compiler_params=grant(12),
    )(group, cross, flag, stepped.reshape(z.members, z.pitch, LANES), part, tapers, wet)
    sums = exchange(sums)
    sums = [sums] + [swap(z, sums, x) for x in slots]
    padded = z.states + -z.states % SUBS
    weight, shift = pl.pallas_call(
        functools.partial(weights_kernel, z),
        in_specs=[smem()] + [vmem] * (z.groups_m + 3),
        out_specs=[vmem] * 2,
        out_shape=[struct(z.members, 3 * n, dtype=BF16), struct(padded, LANES)],
        name="weights",
        compiler_params=grant(8),
    )(index, *sums, lift, relay, gap)
    sems = pltpu.SemaphoreType.DMA((z.groups_m, z.chunks, z.groups))
    result = pl.pallas_call(
        functools.partial(update_kernel, z),
        in_specs=[smem()] * 3 + [vmem] * (z.groups_m + 5),
        out_specs=hbm,
        out_shape=struct(z.members, z.lines, LANES),
        scratch_shapes=[
            VMEM((z.members, z.chunk_pitch, LANES), F32),
            VMEM((z.chunks, z.members, z.chunk_pitch, LANES), F32),
            work,
            gains,
            sems,
        ],
        name="update",
        compiler_params=grant(20),
    )(group, cross, flag, stepped, *moved, gain, tapers, wet, weight, shift)
    result = result.reshape(z.members, z.fields, z.levels, z.col_tiles, z.block_rows, LANES)
    result = jnp.swapaxes(result, 3, 4)
    return result.reshape(z.members, z.fields, z.levels, z.block_rows, z.cols)


def solution(mesh):
    in_specs = (
        P("member", None, None, None, "domain"),
        P(None, None, None, "domain"),
        P(),
        P(None, "domain"),
        P(),
        P(),
        P(),
        P(),
    )
    out_specs = P(None, None, None, "member", "domain")
    return jax.shard_map(local, mesh=mesh, in_specs=in_specs, out_specs=out_specs, check_vma=False)
```
